256 devices in a mesh: row: 32 (over z, x), layer: 8 (over y, core).
Axes of the slice: x: 4, y: 4, z: 8, core: 2. Of those that a mesh axis runs over, the one named last changes fastest.
Arguments:
- window_points: int32 [2, 32768], P(None, 'row'), may hold values from 0 to 63
- pivot_points: int32 [2, 512], replicated, may hold values from 0 to 63
- window_factor: bfloat16 [32768, 16384], P('row', 'layer'), may hold values from -1.5 to 1.5
- pivot_factor: bfloat16 [512, 16384], P('row', 'layer'), may hold values from -0.0234375 to 0.0234375
- right_sides: bfloat16 [32768, 512], P('row', 'layer'), may hold values from -6 to 6
- pivot_sides: bfloat16 [512, 512], P('row', 'layer'), may hold values from -6 to 6
Outputs:
- panel_factor: float32 [32768, 512], P('row', 'layer')
- eliminated: float32 [32768, 512], P('row', 'layer')
The draws below stay inside these ranges and needn't reach their ends.
All inputs are finite; a program needn't handle non-finite values.
Results may differ from the reference program's by a relative error of at most 0.0006.
Values may be sent and summed in bfloat16 or wider, within the bound.
No kernel may reach another device: no remote copies, remote signals or barrier semaphores. Data moves between devices by JAX's collectives and lax.ppermute only.
A program may use at most 64 MiB of HBM per device.

```python
import jax
import jax.numpy as jnp
from jax import lax

K = 16384
P_SIZE = 512
NRHS = 512
GRID = 64
WIN = 32768


def place_ends(array, own_key, smallest, largest):
    dims = array.shape
    spot = [jax.random.randint(jax.random.fold_in(own_key, axis), (), 0, dims[axis]) for axis in range(len(dims))]
    array = array.at[tuple(spot)].set(smallest)
    longest = dims.index(max(dims))
    spot[longest] = (spot[longest] + 1) % dims[longest]
    return array.at[tuple(spot)].set(largest)


def level_of(own_key, shape, cuts, smallest, top_value):
    def one(axis_at, parts):
        heights = jax.random.uniform(jax.random.fold_in(jax.random.fold_in(own_key, 6), axis_at), (parts,), jnp.float32, smallest / len(cuts), top_value / len(cuts))
        return jnp.repeat(jnp.exp(heights), shape[axis_at] // parts).reshape((-1,) + (1,) * (len(shape) - axis_at - 1))

    gain = one(*cuts[0])
    for cut in cuts[1:]:
        gain = gain * one(*cut)
    return gain


def gaussian(rng, extent, deviation, reach, cuts=(), held_as=jnp.bfloat16):
    result = jax.random.normal(rng, extent, jnp.float32) * deviation
    if len(cuts) > 0:
        result = level_of(rng, extent, cuts, -0.22, 0.18) * result
    return jnp.clip(result, min=-reach, max=reach).astype(held_as)


def setup_inputs(seed: int = 0) -> dict:
    key_list = jax.random.split(jax.random.key(seed), 7)
    window_points = place_ends(jax.random.randint(key_list[0], (2, WIN), 0, GRID), jax.random.fold_in(key_list[0], 1), 0, GRID - 1).astype(jnp.int32)
    pivot_points = place_ends(jax.random.randint(key_list[1], (2, P_SIZE), 0, GRID), jax.random.fold_in(key_list[1], 1), 0, GRID - 1).astype(jnp.int32)
    window_factor = gaussian(key_list[2], (WIN, K), (max(K // 1024, 1)) ** -0.5, 1.5, ((0, 32), (1, 8)))
    pivot_factor = gaussian(key_list[3], (P_SIZE, K), (4 * K) ** -0.5, 0.0234375, ((0, 32), (1, 8)))
    right_sides = gaussian(key_list[4], (WIN, NRHS), 1.0, 6.0, ((0, 32), (1, 8)))
    pivot_sides = gaussian(key_list[5], (P_SIZE, NRHS), 1.0, 6.0, ((0, 32), (1, 8)))
    return dict(window_points=window_points, pivot_points=pivot_points, window_factor=window_factor, pivot_factor=pivot_factor, right_sides=right_sides, pivot_sides=pivot_sides)


nugget_value = 2.0
variance_value = 4.0
length_scale = 4.0

def matern(first_points, second_points):
    first_float = first_points.astype(jnp.float32)
    second_float = second_points.astype(jnp.float32)
    delta_x = first_float[0][:, None] - second_float[0][None, :]
    delta_y = first_float[1][:, None] - second_float[1][None, :]
    scaled = jnp.sqrt(delta_x * delta_x + delta_y * delta_y) * (jnp.sqrt(3.0) / length_scale)
    return variance_value * (1.0 + scaled) * jnp.exp(-scaled)

def reference(window_points, pivot_points, window_factor, pivot_factor, right_sides, pivot_sides):
    schur_sum = lax.dot_general(window_factor.astype(jnp.float32), pivot_factor.astype(jnp.float32), (((1,), (1,)), ((), ())), preferred_element_type=jnp.float32)
    gram_sum = lax.dot_general(pivot_factor.astype(jnp.float32), pivot_factor.astype(jnp.float32), (((1,), (1,)), ((), ())), preferred_element_type=jnp.float32)
    count = pivot_points.shape[1]
    diagonal_block = matern(pivot_points, pivot_points) + nugget_value * jnp.eye(count, dtype=jnp.float32) - gram_sum
    factor = jnp.linalg.cholesky(diagonal_block)
    panel_block = matern(window_points, pivot_points) - schur_sum
    solved = jax.scipy.linalg.solve_triangular(factor, panel_block.T, lower=True).T
    reduced = jax.scipy.linalg.solve_triangular(factor, pivot_sides.astype(jnp.float32), lower=True)
    eliminated = right_sides.astype(jnp.float32) - jnp.dot(solved, reduced, precision=lax.Precision.HIGHEST)
    return (solved, eliminated)
```

```python
import jax
import jax.numpy as jnp
from jax import lax
from jax.experimental import pallas as pl
from jax.experimental.pallas import tpu as pltpu
from jax.sharding import PartitionSpec as P

nugget_value = 2.0
variance_value = 4.0
length_scale = 4.0


F32 = jnp.float32
BF16 = jnp.bfloat16
NN = ((1,), (0,))
NT = ((1,), (1,))
TN = ((0,), (0,))

NX, NZ, NY, NC = 4, 8, 4, 2
COUNT = 512
STEP = 64
BLOCKS = [(i, j) for i in range(4) for j in range(i + 1)]


def shift_x(k):
    return [(z * NX + x, z * NX + (x + k) % NX) for z in range(NZ) for x in range(NX)]


def shift_z(k):
    return [(z * NX + x, (z + k) % NZ * NX + x) for z in range(NZ) for x in range(NX)]


def shift_y(k):
    return [(y * NC + c, (y + k) % NY * NC + c) for y in range(NY) for c in range(NC)]


SWAP = [(y * NC + c, y * NC + 1 - c) for y in range(NY) for c in range(NC)]


def place():
    row, layer = lax.axis_index("row"), lax.axis_index("layer")
    return row // NX, lax.rem(row, NX), layer // NC, lax.rem(layer, NC)


def matern(first_points, second_points):
    first_float = first_points.astype(F32)
    second_float = second_points.astype(F32)
    delta_x = first_float[0][:, None] - second_float[0][None, :]
    delta_y = first_float[1][:, None] - second_float[1][None, :]
    scaled = jnp.sqrt(delta_x * delta_x + delta_y * delta_y) * (jnp.sqrt(3.0) / length_scale)
    return variance_value * (1.0 + scaled) * jnp.exp(-scaled)


def product(a, b, dims):
    return lax.dot_general(a, b, (dims, ((), ())), precision=lax.Precision.HIGHEST, preferred_element_type=F32)


def halves_product(a, b, dims):
    one = lambda u, v: lax.dot_general(u, v, (dims, ((), ())), preferred_element_type=F32)
    a_up, b_up = a.astype(BF16), b.astype(BF16)
    a_low = (a - a_up.astype(F32)).astype(BF16)
    b_low = (b - b_up.astype(F32)).astype(BF16)
    return one(a_low, b_up) + one(a_up, b_low) + one(a_up, b_up)


LEFT, RIGHT = 1024, 1152
WIDE = LEFT + RIGHT


def gather_rows(left, right):
    hop = lambda a, perm: lax.ppermute(a, "row", perm)
    near = [left] + [hop(left, shift_x(k)) for k in (1, 2, 3)]
    right_z = [right] + [hop(right, shift_z(k)) for k in range(1, NZ)]
    group = jnp.concatenate(near, axis=0)
    up1, down1 = hop(group, shift_z(1)), hop(group, shift_z(-1))
    up2, down2 = hop(group, shift_z(2)), hop(group, shift_z(-2))
    up3, down3 = hop(up2, shift_z(1)), hop(down2, shift_z(-1))
    up4, down4 = hop(up2[:32], shift_z(2)), hop(down2[32:], shift_z(-2))
    tower = jnp.concatenate(right_z, axis=0)
    side = [tower] + [hop(tower, shift_x(k)) for k in (1, 2, 3)]
    return (group, up1, down1, up2, down2, up3, down3, up4, down4), side


def gram_kernel(group, up1, down1, up2, down2, up3, down3, up4, down4, side0, side1, side2, side3, rows, other, mine, blocks, sem):
    z, x, y, c = place()

    def put(piece, start, z_from, x_from, first, width, which):
        at = pl.multiple_of((lax.rem(z_from + 2 * NZ, NZ) * NX + lax.rem(x_from + NX, NX)) * 16, 16)
        pltpu.make_async_copy(piece.at[start : start + 16], rows.at[pl.ds(at, 16), first : first + width], sem.at[which]).start()

    for piece, shift, first in (
        (group, 0, 0), (up1, -1, 0), (down1, 1, 0), (up2, -2, 0), (down2, 2, 0), (up3, -3, 0), (down3, 3, 0), (up4, -4, 0), (down4, 4, 2),
    ):
        for i in range(piece.shape[0] // 16):
            put(piece, 16 * i, z + shift, x - (first + i), 0, LEFT, 0)
    for k, piece in enumerate((side0, side1, side2, side3)):
        for i in range(NZ):
            put(piece, 16 * i, z - i, x - k, LEFT, RIGHT, 1)
    pltpu.make_async_copy(rows.at[:, :LEFT], rows.at[:, :LEFT], sem.at[0]).wait()
    pltpu.make_async_copy(rows.at[:, LEFT:], rows.at[:, LEFT:], sem.at[1]).wait()

    at = 0
    for i in range(4):
        part = lax.dot_general(
            rows[128 * i : 128 * i + 128, :2048], rows[: 128 * i + 128, :2048], (NT, ((), ())), preferred_element_type=F32
        )
        for j in range(i + 1):
            blocks[at] = part[:, 128 * j : 128 * j + 128]
            at += 1
    for k in range(NY):
        for out, core in ((other, 1 - c), (mine, c)):
            first = pl.multiple_of(64 * core + 16 * lax.rem(y + k, NY), 16)
            for b in range(len(BLOCKS)):
                out[k, 16 * b : 16 * b + 16] = blocks[b, pl.ds(first, 16), :]


def gram(left_pieces, right_pieces):
    chunk = jax.ShapeDtypeStruct((NY, 16 * len(BLOCKS), 128), F32)
    return pl.pallas_call(
        gram_kernel,
        name="gram",
        out_shape=(jax.ShapeDtypeStruct((COUNT, WIDE), BF16), chunk, chunk),
        in_specs=[pl.BlockSpec(memory_space=pl.ANY)] * 13,
        scratch_shapes=[pltpu.VMEM((len(BLOCKS), 128, 128), F32), pltpu.SemaphoreType.DMA((2,))],
        cost_estimate=pl.CostEstimate(flops=2 * COUNT * COUNT * 2048, bytes_accessed=3 << 20, transcendentals=0),
    )(*left_pieces, *right_pieces)


def schur_kernel(order, window, rows, out):
    out[0] = lax.dot_general(window[...], rows[:, :2048], (NT, ((), ())), preferred_element_type=F32)


def schur(order, window, rows):
    return pl.pallas_call(
        schur_kernel,
        name="schur",
        out_shape=jax.ShapeDtypeStruct((NY, 128, COUNT), F32),
        grid_spec=pltpu.PrefetchScalarGridSpec(
            num_scalar_prefetch=1,
            grid=(NY,),
            in_specs=[
                pl.BlockSpec((128, 2048), lambda i, order: (order[i], 0)),
                pl.BlockSpec((COUNT, WIDE), lambda i, order: (0, 0)),
            ],
            out_specs=pl.BlockSpec((1, 128, COUNT), lambda i, order: (i, 0, 0)),
        ),
        cost_estimate=pl.CostEstimate(flops=2 * COUNT * COUNT * 2048, bytes_accessed=5 << 20, transcendentals=0),
    )(order, window, rows)


def invert_factor(block):
    lane = lax.broadcasted_iota(jnp.int32, (STEP, STEP), 1)
    sub = lax.broadcasted_iota(jnp.int32, (STEP, STEP), 0)
    both = jnp.concatenate([block, jnp.where(lane == sub, 1.0, 0.0).astype(F32)], axis=1)
    a = [both[8 * g : 8 * g + 8] for g in range(8)]
    row = lax.broadcasted_iota(jnp.int32, (8, 128), 0)
    spread = lambda v, j: jnp.broadcast_to(v[j : j + 1], (8, 128))
    done = []
    for p in range(8):
        column = {
            (c, g): jnp.broadcast_to(a[g][:, 8 * p + c : 8 * p + c + 1], (8, 128)) for g in range(p, 8) for c in range(8)
        }
        pivots = jnp.ones((8, 128), F32)
        for j in range(8):
            d = spread(column[j, p], j)
            pivots = jnp.where(row == j, d, pivots)
            r = 1.0 / d
            lead = spread(a[p], j)
            heads = {c: spread(column[c, p], j) for c in range(j + 1, 8)}
            for g in range(p, 8):
                m = column[j, g]
                if g == p:
                    m = jnp.where(row > j, m, 0.0)
                for c in range(j + 1, 8):
                    column[c, g] = column[c, g] - (m * heads[c]) * r
                a[g] = a[g] - (m * lead) * r
        done.append(a[p] * lax.rsqrt(pivots))
    return jnp.concatenate(done, axis=0)[:, STEP:]


def factor_kernel(cov, sides, own, near1, near2, near3, far, weights, a, e):
    z, x, y, c = place()
    layer = lax.axis_index("layer")
    for k in range(NY):
        for core in range(NC):
            piece = (own, near1, near2, near3)[k] if core == 0 else far.at[k]
            which = c if core == 0 else 1 - c
            first = pl.multiple_of(64 * which + 16 * lax.rem(y - k + NY, NY), 16)
            for b, (i, j) in enumerate(BLOCKS):
                at = (pl.ds(128 * i + first, 16), slice(128 * j, 128 * j + 128))
                a[at] = cov[at] - piece[16 * b : 16 * b + 16]
    e[...] = jnp.zeros_like(e)

    b = STEP
    block = a[0:b, 0:b]
    for k in range(COUNT // b):
        lo = k * b
        hi = lo + b
        nx = hi + b
        t = invert_factor(block)
        inverse = t if k == 0 else jnp.concatenate([product(t, e[lo:hi, :lo], NN), t], axis=1)
        e[lo:hi, :hi] = inverse
        if hi == COUNT:
            break
        below = product(a[hi:nx, lo:hi], t, NT)
        block = a[hi:nx, hi:nx] - product(below, below, NT)
        if k > 0:
            e[hi:nx, :lo] = e[hi:nx, :lo] - product(below, inverse[:, :lo], NN)
        e[hi:nx, lo:hi] = -product(below, t, NN)
        if nx < COUNT:
            rest = product(a[nx:, lo:hi], t, NT)
            a[nx:, hi:nx] = a[nx:, hi:nx] - product(rest, below, NT)
            a[nx:, nx:] = a[nx:, nx:] - product(rest, rest, NT)
            if k > 0:
                e[nx:, :lo] = e[nx:, :lo] - product(rest, inverse[:, :lo], NN)
            e[nx:, lo:hi] = -product(rest, t, NN)

    reduced = product(e[...], sides[:, :64].astype(F32), NN)
    weights[0:64, :] = e[pl.ds(pl.multiple_of(64 * layer, 64), 64), :]
    weights[64:128, :] = product(reduced, e[...], TN)


def factor(cov, sides, own, near1, near2, near3, far):
    return pl.pallas_call(
        factor_kernel,
        name="factor",
        out_shape=jax.ShapeDtypeStruct((128, COUNT), F32),
        scratch_shapes=[pltpu.VMEM((COUNT, COUNT), F32), pltpu.VMEM((COUNT, COUNT), F32)],
        cost_estimate=pl.CostEstimate(flops=4 * 10**9, bytes_accessed=3 << 20, transcendentals=0),
    )(cov, sides, own, near1, near2, near3, far)


def finish_kernel(weights, near, far, sides, panel, rest):
    z, x, y, c = place()
    k = pl.program_id(0)
    for piece, core in ((near, c), (far, 1 - c)):
        at = pl.multiple_of(512 * core + 128 * lax.rem(y - k + NY, NY), 128)
        both = halves_product(weights[...], piece[0], NT)
        panel[:, pl.ds(at, 128)] = both[:64]
        rest[:, pl.ds(at, 128)] = sides[:, pl.ds(at, 128)].astype(F32) - both[64:]


def finish(weights, near, far, sides):
    whole = lambda shape: pl.BlockSpec(shape, lambda k: (0, 0))
    piece = pl.BlockSpec((1, 128, COUNT), lambda k: (k, 0, 0))
    return pl.pallas_call(
        finish_kernel,
        name="finish",
        grid=(NY,),
        out_shape=(jax.ShapeDtypeStruct((64, 1024), F32),) * 2,
        in_specs=[whole((128, COUNT)), piece, piece, whole((64, 1024))],
        out_specs=(whole((64, 1024)),) * 2,
        cost_estimate=pl.CostEstimate(flops=6 * 1024 * 512 * 128, bytes_accessed=3 << 20, transcendentals=0),
    )(weights, near, far, sides)


def shards(window_points, pivot_points, window_factor, pivot_factor, right_sides, pivot_sides):
    z, x, y, c = place()
    swap = lambda a: lax.ppermute(a, "layer", SWAP)
    along = lambda a, k: lax.ppermute(a, "layer", shift_y(k))

    left = pivot_factor[:, :LEFT]
    right = jnp.concatenate([pivot_factor[:, LEFT:], pivot_sides, jnp.zeros_like(pivot_sides)], axis=1)
    left_pieces, right_pieces = gather_rows(left, right)
    rows, gram_other, gram_mine = gram(left_pieces, right_pieces)

    gram_far = swap(gram_other)
    gram_sum = [gram_mine[k] + gram_far[k] for k in range(NY)]
    gram_in = [along(gram_sum[k], k) for k in (1, 2, 3)]
    gram_own = gram_sum[0] + (gram_in[0] + gram_in[1] + gram_in[2])
    gram_near = [gram_own] + [along(gram_own, k) for k in (1, 2, 3)]
    gram_far = swap(jnp.stack(gram_near))

    cov = matern(pivot_points, pivot_points) + nugget_value * jnp.eye(COUNT, dtype=F32)

    turn = lax.rem(y + jnp.arange(NY, dtype=jnp.int32), NY)
    schur_other = schur(NY * (1 - c) + turn, window_factor, rows)
    schur_mine = schur(NY * c + turn, window_factor, rows)
    schur_far = swap(schur_other)
    schur_sum = [schur_mine[k] + schur_far[k] for k in range(NY)]
    schur_in = [along(schur_sum[k], k) for k in (1, 2, 3)]
    points = lax.dynamic_slice_in_dim(window_points, 512 * c + 128 * y, 128, 1)
    panel_own = matern(points, pivot_points) - (schur_sum[0] + (schur_in[0] + schur_in[1] + schur_in[2]))
    panel_near = jnp.stack([panel_own] + [along(panel_own, k) for k in (1, 2, 3)])
    panel_far = swap(panel_near)

    weights = factor(cov, rows[:, 2048:], *gram_near, gram_far)
    panel, rest = finish(weights, panel_near, panel_far, right_sides.T)
    return panel.T, rest.T


def solution(mesh):
    placed = (
        P(None, "row"),
        P(),
        P("row", "layer"),
        P("row", "layer"),
        P("row", "layer"),
        P("row", "layer"),
    )
    return jax.shard_map(
        shards,
        mesh=mesh,
        in_specs=placed,
        out_specs=(P("row", "layer"), P("row", "layer")),
        check_vma=False,
    )
```

```python
import jax
import jax.numpy as jnp
from jax import lax
from jax.experimental import pallas as pl
from jax.experimental.pallas import tpu as pltpu
from jax.sharding import PartitionSpec as P


nugget_value = 2.0
variance_value = 4.0
length_scale = 4.0


F32 = jnp.float32
BF16 = jnp.bfloat16
NN = ((1,), (0,))
NT = ((1,), (1,))
TN = ((0,), (0,))

NX, NZ, NY, NC = 4, 8, 4, 2
COUNT = 512
STEP = 64
BLOCKS = [(i, j) for i in range(4) for j in range(i + 1)]


def shift_x(k):
    return [(z * NX + x, z * NX + (x + k) % NX) for z in range(NZ) for x in range(NX)]


def shift_z(k):
    return [(z * NX + x, (z + k) % NZ * NX + x) for z in range(NZ) for x in range(NX)]


def shift_y(k):
    return [(y * NC + c, (y + k) % NY * NC + c) for y in range(NY) for c in range(NC)]


SWAP = [(y * NC + c, y * NC + 1 - c) for y in range(NY) for c in range(NC)]


def place():
    row, layer = lax.axis_index("row"), lax.axis_index("layer")
    return row // NX, lax.rem(row, NX), layer // NC, lax.rem(layer, NC)


def matern(first_points, second_points):
    first_float = first_points.astype(F32)
    second_float = second_points.astype(F32)
    delta_x = first_float[0][:, None] - second_float[0][None, :]
    delta_y = first_float[1][:, None] - second_float[1][None, :]
    scaled = jnp.sqrt(delta_x * delta_x + delta_y * delta_y) * (jnp.sqrt(3.0) / length_scale)
    return variance_value * (1.0 + scaled) * jnp.exp(-scaled)


def product(a, b, dims):
    return lax.dot_general(a, b, (dims, ((), ())), precision=lax.Precision.HIGHEST, preferred_element_type=F32)


def upper_lower(a):
    up = a.astype(BF16)
    return up, (a - up.astype(F32)).astype(BF16)


def halves_product(a_up, a_low, b):
    one = lambda u, v: lax.dot_general(u, v, (NT, ((), ())), preferred_element_type=F32)
    b_up, b_low = upper_lower(b)
    return one(a_low, b_up) + one(a_up, b_low) + one(a_up, b_up)


HELD = 2048 + 128
VMEM = pl.BlockSpec(memory_space=pltpu.VMEM)


def grant(mib):
    return pltpu.CompilerParams(vmem_limit_bytes=mib << 20)


LEFT = 1024
PIECES = ((0, 0), (-1, 0), (1, 0), (-2, 0), (2, 0), (-3, 0), (3, 0), (4, 0), (4, 2))


def rings(parts):
    pieces = [[own] for own in parts]
    for turn in range(1, 5):
        for held in pieces:
            up, down = (held[0], held[0]) if turn == 1 else held[-2:]
            if turn == 4:
                up, down = up[:32], down[32:]
            held.append(lax.ppermute(up, "row", shift_z(1)))
            held.append(lax.ppermute(down, "row", shift_z(-1)))
    return pieces


def stack_kernel(near0, near1, near2, near3, left, right):
    for i, piece in enumerate((near0, near1, near2, near3)):
        left[16 * i : 16 * i + 16] = piece[:, :LEFT]
        right[16 * i : 16 * i + 16] = piece[:, LEFT:]


def stack(near):
    return pl.pallas_call(
        stack_kernel,
        name="stack",
        out_shape=(jax.ShapeDtypeStruct((64, LEFT), BF16), jax.ShapeDtypeStruct((64, HELD - LEFT), BF16)),
        in_specs=[VMEM] * 4,
        out_specs=(VMEM, VMEM),
        compiler_params=grant(2),
        cost_estimate=pl.CostEstimate(flops=10**6, bytes_accessed=1 << 19, transcendentals=0),
    )(*near)


def gram_kernel(*refs):
    left, right, (rows, sides, other, mine, blocks) = refs[:9], refs[9:18], refs[18:]
    z, x, y, c = place()
    for one, two, (turn, first) in zip(left, right, PIECES):
        for i in range(one.shape[0] // 16):
            at = (lax.rem(z + turn + NZ, NZ) * NX + lax.rem(x - first - i + NX, NX)) * 16
            at = pl.ds(pl.multiple_of(at, 16), 16)
            rows[at, :LEFT] = one[16 * i : 16 * i + 16]
            rows[at, LEFT:] = two[16 * i : 16 * i + 16, : 2048 - LEFT]
            sides[at] = two[16 * i : 16 * i + 16, 2048 - LEFT :]
    at = 0
    for i in range(4):
        part = lax.dot_general(
            rows[128 * i : 128 * i + 128], rows[: 128 * i + 128], (NT, ((), ())), preferred_element_type=F32
        )
        for j in range(i + 1):
            blocks[at] = part[:, 128 * j : 128 * j + 128]
            at += 1
    for k in range(NY):
        for out, core in ((other, 1 - c), (mine, c)):
            first = pl.multiple_of(64 * core + 16 * lax.rem(y + k, NY), 16)
            for b in range(len(BLOCKS)):
                out[k, 16 * b : 16 * b + 16] = blocks[b, pl.ds(first, 16), :]


def gram(left, right):
    chunk = jax.ShapeDtypeStruct((NY, 16 * len(BLOCKS), 128), F32)
    return pl.pallas_call(
        gram_kernel,
        name="gram",
        out_shape=(
            jax.ShapeDtypeStruct((COUNT, 2048), BF16),
            jax.ShapeDtypeStruct((COUNT, 128), BF16),
            chunk,
            chunk,
        ),
        in_specs=[VMEM] * 18,
        out_specs=(VMEM,) * 4,
        scratch_shapes=[pltpu.VMEM((len(BLOCKS), 128, 128), F32)],
        compiler_params=grant(10),
        cost_estimate=pl.CostEstimate(flops=2 * COUNT * COUNT * 2048, bytes_accessed=2 << 20, transcendentals=0),
    )(*left, *right)


def schur_kernel(window, rows, other, mine, held, sem):
    _, _, y, c = place()

    def fetch(i):
        slot = lax.rem(i, 2)
        core = jnp.where(i < 2, 1 - c, c)
        first = pl.multiple_of(512 * core + 256 * slot, 256)
        return pltpu.make_async_copy(window.at[pl.ds(first, 256)], held.at[slot], sem.at[slot])

    fetch(0).start()

    @pl.loop(0, 4)
    def _(i):
        @pl.when(i < 3)
        def _():
            fetch(i + 1).start()

        fetch(i).wait()
        part = lax.dot_general(held[lax.rem(i, 2)], rows[...], (NT, ((), ())), preferred_element_type=F32)
        for n in range(2):
            k = lax.rem(2 * lax.rem(i, 2) + n - y + NY, NY)

            @pl.when(i < 2)
            def _():
                other[k] = part[128 * n : 128 * n + 128]

            @pl.when(i >= 2)
            def _():
                mine[k] = part[128 * n : 128 * n + 128]


def schur(window, rows):
    chunk = jax.ShapeDtypeStruct((NY, 128, COUNT), F32)
    return pl.pallas_call(
        schur_kernel,
        name="schur",
        out_shape=(chunk, chunk),
        in_specs=[pl.BlockSpec(memory_space=pltpu.HBM), VMEM],
        out_specs=(VMEM, VMEM),
        scratch_shapes=[pltpu.VMEM((2, 256, 2048), BF16), pltpu.SemaphoreType.DMA((2,))],
        compiler_params=grant(12),
        cost_estimate=pl.CostEstimate(flops=2 * 1024 * COUNT * 2048, bytes_accessed=8 << 20, transcendentals=0),
    )(window, rows)


def tree_sum(terms):
    terms = list(terms)
    while len(terms) > 1:
        terms = [terms[i] + terms[i + 1] if i + 1 < len(terms) else terms[i] for i in range(0, len(terms), 2)]
    return terms[0]


def invert_factor(block):
    lane = lax.broadcasted_iota(jnp.int32, (STEP, STEP), 1)
    sub = lax.broadcasted_iota(jnp.int32, (STEP, STEP), 0)
    both = jnp.concatenate([block, jnp.where(lane == sub, 1.0, 0.0).astype(F32)], axis=1)
    a = [both[8 * g : 8 * g + 8] for g in range(8)]
    row = lax.broadcasted_iota(jnp.int32, (8, 128), 0)
    spread = lambda v, j: jnp.broadcast_to(v[j : j + 1], (8, 128))
    lanes = lambda v, j: jnp.broadcast_to(v[:, j : j + 1], (8, 128))
    done = []
    column = [lanes(a[0], c) for c in range(8)]
    for p in range(8):
        more = p + 1 < 8
        if more:
            below = [lanes(a[p + 1], 8 * p + 8 + c) for c in range(8)]
            right = [lanes(a[p], 8 * p + 8 + c) for c in range(8)]
        old = {(c, g): lanes(a[g], 8 * p + c) for g in range(p + 1, 8) for c in range(8)}
        factor_rows = solved_rows = a[p]
        pivots = jnp.ones((8, 128), F32)
        scale = pivots
        for j in range(8):
            d = spread(column[j], j)
            r = 1.0 / d
            full = jnp.where(row != j, column[j], 0.0)
            low = jnp.where(row > j, column[j], 0.0)
            full_r = full * r
            lead = spread(factor_rows, j) * r
            for c in range(j + 1, 8):
                if c == j + 1:
                    column[c] = column[c] - (full * spread(column[c], j)) * r
                else:
                    column[c] = column[c] - full_r * spread(column[c], j)
            if more:
                right = [v - full_r * spread(v, j) for v in right]
            solved_rows = solved_rows - full * lead
            factor_rows = factor_rows - low * lead
            pivots = jnp.where(row == j, d, pivots)
            scale = jnp.where(row == j, r, scale)
        done.append(factor_rows * lax.rsqrt(pivots))
        if more:
            right = [v * scale for v in right]
            column = [below[c] - tree_sum(old[k, p + 1] * spread(right[c], k) for k in range(8)) for c in range(8)]
        solved_rows = solved_rows * scale
        heads = [spread(solved_rows, c) for c in range(8)]
        for g in range(p + 1, 8):
            a[g] = a[g] - tree_sum(old[c, g] * heads[c] for c in range(8))
    return jnp.concatenate(done, axis=0)[:, STEP:]


def factor_steps(a, e, block, half, cross, first):
    b, w = STEP, 128

    def upper(k):
        lo = k * w
        mid, hi = lo + b, lo + w
        t1 = half[...]
        inner = product(a[mid:hi, lo:mid], t1, NT)
        block[...] = a[mid:hi, mid:hi] - product(inner, inner, NT)
        e[lo:mid, lo:mid] = t1
        cross[...] = product(inner, t1, NN)

    def lower(k):
        lo = k * w
        mid, hi, nx = lo + b, lo + w, lo + 2 * w
        t2 = half[...]
        e[mid:hi, lo:mid] = -product(t2, cross[...], NN)
        e[mid:hi, mid:hi] = t2
        t = e[lo:hi, lo:hi]
        if hi < COUNT:
            below = product(a[hi:nx, lo:hi], t, NT)
            square = a[hi:nx, hi:nx] - product(below, below, NT)
            a[hi:nx, hi:nx] = square
            block[...] = square[:b, :b]
        if k > 0:
            left = product(t, e[lo:hi, :lo], NN)
            e[lo:hi, :lo] = left
        if hi < COUNT:
            if k > 0:
                e[hi:nx, :lo] = e[hi:nx, :lo] - product(below, left, NN)
            e[hi:nx, lo:hi] = -product(below, t, NN)
            if nx < COUNT:
                rest = product(a[nx:, lo:hi], t, NT)
                a[nx:, hi:nx] = a[nx:, hi:nx] - product(rest, below, NT)
                a[nx:, nx:] = a[nx:, nx:] - product(rest, rest, NT)
                if k > 0:
                    e[nx:, :lo] = e[nx:, :lo] - product(rest, left, NN)
                e[nx:, lo:hi] = -product(rest, t, NN)

    @pl.loop(0, 4)
    def _(i):
        half[...] = invert_factor(block[...])
        for n, (part, k) in enumerate(((upper, first), (lower, first), (upper, first + 1), (lower, first + 1))):
            pl.when(i == n)(lambda part=part, k=k: part(k))


STEPS_SCRATCH = [pltpu.VMEM((STEP, STEP), F32)] * 3


def factor_kernel(cov, own, near1, near2, near3, far, a, e, block, half, cross):
    _, _, y, c = place()
    for k in range(NY):
        for core in range(NC):
            piece = (own, near1, near2, near3)[k] if core == 0 else far.at[k]
            which = c if core == 0 else 1 - c
            first = pl.multiple_of(64 * which + 16 * lax.rem(y - k + NY, NY), 16)
            for b, (i, j) in enumerate(BLOCKS):
                at = (pl.ds(128 * i + first, 16), slice(128 * j, 128 * j + 128))
                a[at] = cov[at] - piece[16 * b : 16 * b + 16]
    e[...] = jnp.zeros_like(e)
    block[...] = a[:STEP, :STEP]
    factor_steps(a, e, block, half, cross, 0)


def factor(*args):
    square = jax.ShapeDtypeStruct((COUNT, COUNT), F32)
    return pl.pallas_call(
        factor_kernel,
        name="factor",
        out_shape=(square, square),
        in_specs=[VMEM] * 6,
        out_specs=(VMEM, VMEM),
        scratch_shapes=STEPS_SCRATCH,
        compiler_params=grant(10),
        cost_estimate=pl.CostEstimate(flops=10**10, bytes_accessed=4 << 20, transcendentals=0),
    )(*args)


def weights_kernel(a_in, e_in, sides, a, e, weights, block, half, cross):
    layer = lax.axis_index("layer")
    block[...] = a[256 : 256 + STEP, 256 : 256 + STEP]
    factor_steps(a, e, block, half, cross, 2)
    reduced = product(e[...], sides[:, :64].astype(F32), NN)
    weights[:64] = e[pl.ds(pl.multiple_of(64 * layer, 64), 64), :]
    weights[64:] = product(reduced, e[...], TN)


def weigh(a, e, sides):
    square = jax.ShapeDtypeStruct((COUNT, COUNT), F32)
    return pl.pallas_call(
        weights_kernel,
        name="weigh",
        out_shape=(square, square, jax.ShapeDtypeStruct((128, COUNT), F32)),
        in_specs=[VMEM] * 3,
        out_specs=(VMEM,) * 3,
        scratch_shapes=STEPS_SCRATCH,
        input_output_aliases={0: 0, 1: 1},
        compiler_params=grant(10),
        cost_estimate=pl.CostEstimate(flops=10**10, bytes_accessed=4 << 20, transcendentals=0),
    )(a, e, sides)[2]


def finish_kernel(weights, near, far, sides, panel, rest):
    _, _, y, c = place()
    up, low = upper_lower(weights[...])
    for piece, core in ((near, c), (far, 1 - c)):

        @pl.loop(0, NY)
        def _(k):
            at = pl.multiple_of(512 * core + 128 * lax.rem(y - k + NY, NY), 128)
            both = halves_product(up, low, piece[k])
            panel[:, pl.ds(at, 128)] = both[:64]
            rest[:, pl.ds(at, 128)] = sides[:, pl.ds(at, 128)].astype(F32) - both[64:]


def finish(*args):
    return pl.pallas_call(
        finish_kernel,
        name="finish",
        out_shape=(jax.ShapeDtypeStruct((64, 1024), F32),) * 2,
        in_specs=[VMEM] * 4,
        out_specs=(VMEM, VMEM),
        compiler_params=grant(12),
        cost_estimate=pl.CostEstimate(flops=6 * 1024 * 512 * 128, bytes_accessed=3 << 20, transcendentals=0),
    )(*args)


def shards(window_points, pivot_points, window_factor, pivot_factor, right_sides, pivot_sides):
    _, _, y, c = place()
    swap = lambda a: lax.ppermute(a, "layer", SWAP)
    along = lambda a, k: lax.ppermute(a, "layer", shift_y(k))

    held = jnp.concatenate([pivot_factor, pivot_sides, jnp.zeros_like(pivot_sides)], axis=1)
    near = [held] + [lax.ppermute(held, "row", shift_x(k)) for k in (1, 2, 3)]
    left, right = rings(stack(near))
    rows, sides, gram_other, gram_mine = gram(left, right)
    gram_far = swap(gram_other)
    gram_sum = [gram_mine[k] + gram_far[k] for k in range(NY)]
    gram_in = [along(gram_sum[k], k) for k in (1, 2, 3)]
    gram_own = gram_sum[0] + (gram_in[0] + gram_in[1] + gram_in[2])
    gram_near = [gram_own] + [along(gram_own, k) for k in (1, 2, 3)]
    gram_far = swap(jnp.stack(gram_near))

    points = lax.dynamic_slice_in_dim(window_points, 512 * c + 128 * y, 128, 1)
    cov = matern(pivot_points, pivot_points) + nugget_value * jnp.eye(COUNT, dtype=F32)
    covered = matern(points, pivot_points)
    cov, covered = lax.optimization_barrier((cov, covered))
    a, e = factor(cov, *gram_near, gram_far)
    weights = weigh(a, e, sides)

    schur_other, schur_mine = schur(window_factor, rows)
    schur_far = swap(schur_other)
    schur_sum = [schur_mine[k] + schur_far[k] for k in range(NY)]
    schur_in = [along(schur_sum[k], k) for k in (1, 2, 3)]
    panel_own = covered - (schur_sum[0] + (schur_in[0] + schur_in[1] + schur_in[2]))
    panel_near = jnp.stack([panel_own] + [along(panel_own, k) for k in (1, 2, 3)])
    panel_far = swap(panel_near)
    panel, rest = finish(weights, panel_near, panel_far, right_sides.T)
    return panel.T, rest.T


def solution(mesh):
    placed = (
        P(None, "row"),
        P(),
        P("row", "layer"),
        P("row", "layer"),
        P("row", "layer"),
        P("row", "layer"),
    )
    return jax.shard_map(
        shards,
        mesh=mesh,
        in_specs=placed,
        out_specs=(P("row", "layer"), P("row", "layer")),
        check_vma=False,
    )
```

```python
import jax
import jax.numpy as jnp
from jax import lax
from jax.experimental import pallas as pl
from jax.experimental.pallas import tpu as pltpu
from jax.sharding import PartitionSpec as P


nugget_value = 2.0
variance_value = 4.0
length_scale = 4.0


F32 = jnp.float32
BF16 = jnp.bfloat16
NN = ((1,), (0,))
NT = ((1,), (1,))
TN = ((0,), (0,))

NX, NZ, NY, NC = 4, 8, 4, 2
COUNT = 512
STEP = 64
BLOCKS = [(i, j) for i in range(4) for j in range(i + 1)]


def shift_x(k):
    return [(z * NX + x, z * NX + (x + k) % NX) for z in range(NZ) for x in range(NX)]


def shift_z(k):
    return [(z * NX + x, (z + k) % NZ * NX + x) for z in range(NZ) for x in range(NX)]


def shift_y(k):
    return [(y * NC + c, (y + k) % NY * NC + c) for y in range(NY) for c in range(NC)]


SWAP = [(y * NC + c, y * NC + 1 - c) for y in range(NY) for c in range(NC)]


def place():
    row, layer = lax.axis_index("row"), lax.axis_index("layer")
    return row // NX, lax.rem(row, NX), layer // NC, lax.rem(layer, NC)


def matern(first_points, second_points):
    first_float = first_points.astype(F32)
    second_float = second_points.astype(F32)
    delta_x = first_float[0][:, None] - second_float[0][None, :]
    delta_y = first_float[1][:, None] - second_float[1][None, :]
    scaled = jnp.sqrt(delta_x * delta_x + delta_y * delta_y) * (jnp.sqrt(3.0) / length_scale)
    return variance_value * (1.0 + scaled) * jnp.exp(-scaled)


def product(a, b, dims):
    return lax.dot_general(a, b, (dims, ((), ())), precision=lax.Precision.HIGHEST, preferred_element_type=F32)


def upper_lower(a):
    up = a.astype(BF16)
    return up, (a - up.astype(F32)).astype(BF16)


def halves_product(a_up, a_low, b):
    one = lambda u, v: lax.dot_general(u, v, (NT, ((), ())), preferred_element_type=F32)
    b_up, b_low = upper_lower(b)
    return one(a_low, b_up) + one(a_up, b_low) + one(a_up, b_up)


VMEM = pl.BlockSpec(memory_space=pltpu.VMEM)


def grant(mib):
    return pltpu.CompilerParams(vmem_limit_bytes=mib << 20)


PIECES = ((0, 0), (-1, 0), (1, 0), (-2, 0), (2, 0), (-3, 0), (3, 0), (4, 0), (4, 2))


def tower(own):
    hop = lambda a, k: lax.ppermute(a, "row", shift_z(k))
    up1, down1, up2, down2 = hop(own, 1), hop(own, -1), hop(own, 2), hop(own, -2)
    up3, down3 = hop(up2, 1), hop(down2, -1)
    up4, down4 = hop(up2[:32], 2), hop(down2[32:], -2)
    return [own, up1, down1, up2, down2, up3, down3, up4, down4]


def gram_kernel(*refs):
    pieces, (rows, sides, other, mine, blocks) = refs[:9], refs[9:]
    z, x, y, c = place()
    for piece, (turn, first) in zip(pieces, PIECES):

        @pl.loop(0, piece.shape[0] // 16)
        def _(i):
            at = (lax.rem(z + turn + NZ, NZ) * NX + lax.rem(x - first - i + NX, NX)) * 16
            at = pl.ds(pl.multiple_of(at, 16), 16)
            held = piece[pl.ds(pl.multiple_of(16 * i, 16), 16)]
            rows[at] = held[:, :2048]
            sides[at] = held[:, 2048:]

    at = 0
    for i in range(4):
        part = lax.dot_general(
            rows[128 * i : 128 * i + 128], rows[: 128 * i + 128], (NT, ((), ())), preferred_element_type=F32
        )
        for j in range(i + 1):
            blocks[at] = part[:, 128 * j : 128 * j + 128]
            at += 1
    for k in range(NY):
        for out, core in ((other, 1 - c), (mine, c)):
            first = pl.multiple_of(64 * core + 16 * lax.rem(y + k, NY), 16)
            for b in range(len(BLOCKS)):
                out[k, 16 * b : 16 * b + 16] = blocks[b, pl.ds(first, 16), :]


def gram(pieces):
    chunk = jax.ShapeDtypeStruct((NY, 16 * len(BLOCKS), 128), F32)
    return pl.pallas_call(
        gram_kernel,
        name="gram",
        out_shape=(
            jax.ShapeDtypeStruct((COUNT, 2048), BF16),
            jax.ShapeDtypeStruct((COUNT, 128), BF16),
            chunk,
            chunk,
        ),
        in_specs=[VMEM] * 9,
        out_specs=(VMEM,) * 4,
        scratch_shapes=[pltpu.VMEM((len(BLOCKS), 128, 128), F32)],
        compiler_params=grant(10),
        cost_estimate=pl.CostEstimate(flops=2 * COUNT * COUNT * 2048, bytes_accessed=2 << 20, transcendentals=0),
    )(*pieces)


def schur_kernel(window, rows, other, mine, held, sem):
    _, _, y, c = place()

    def fetch(i):
        slot = lax.rem(i, 2)
        core = jnp.where(i < 2, 1 - c, c)
        first = pl.multiple_of(512 * core + 256 * slot, 256)
        return pltpu.make_async_copy(window.at[pl.ds(first, 256)], held.at[slot], sem.at[slot])

    fetch(0).start()

    @pl.loop(0, 4)
    def _(i):
        @pl.when(i < 3)
        def _():
            fetch(i + 1).start()

        fetch(i).wait()
        part = lax.dot_general(held[lax.rem(i, 2)], rows[...], (NT, ((), ())), preferred_element_type=F32)
        for n in range(2):
            k = lax.rem(2 * lax.rem(i, 2) + n - y + NY, NY)

            @pl.when(i < 2)
            def _():
                other[k] = part[128 * n : 128 * n + 128]

            @pl.when(i >= 2)
            def _():
                mine[k] = part[128 * n : 128 * n + 128]


def schur(window, rows):
    chunk = jax.ShapeDtypeStruct((NY, 128, COUNT), F32)
    return pl.pallas_call(
        schur_kernel,
        name="schur",
        out_shape=(chunk, chunk),
        in_specs=[pl.BlockSpec(memory_space=pltpu.HBM), VMEM],
        out_specs=(VMEM, VMEM),
        scratch_shapes=[pltpu.VMEM((2, 256, 2048), BF16), pltpu.SemaphoreType.DMA((2,))],
        compiler_params=grant(12),
        cost_estimate=pl.CostEstimate(flops=2 * 1024 * COUNT * 2048, bytes_accessed=8 << 20, transcendentals=0),
    )(window, rows)


def tree_sum(terms):
    terms = list(terms)
    while len(terms) > 1:
        terms = [terms[i] + terms[i + 1] if i + 1 < len(terms) else terms[i] for i in range(0, len(terms), 2)]
    return terms[0]


def invert_factor(block):
    lane = lax.broadcasted_iota(jnp.int32, (STEP, STEP), 1)
    sub = lax.broadcasted_iota(jnp.int32, (STEP, STEP), 0)
    both = jnp.concatenate([block, jnp.where(lane == sub, 1.0, 0.0).astype(F32)], axis=1)
    a = [both[8 * g : 8 * g + 8] for g in range(8)]
    row = lax.broadcasted_iota(jnp.int32, (8, 128), 0)
    spread = lambda v, j: jnp.broadcast_to(v[j : j + 1], (8, 128))
    lanes = lambda v, j: jnp.broadcast_to(v[:, j : j + 1], (8, 128))
    done = []
    column = [lanes(a[0], c) for c in range(8)]
    for p in range(8):
        more = p + 1 < 8
        if more:
            below = [lanes(a[p + 1], 8 * p + 8 + c) for c in range(8)]
            right = [lanes(a[p], 8 * p + 8 + c) for c in range(8)]
        old = {(c, g): lanes(a[g], 8 * p + c) for g in range(p + 1, 8) for c in range(8)}
        factor_rows = solved_rows = a[p]
        pivots = jnp.ones((8, 128), F32)
        scale = pivots
        for j in range(8):
            d = spread(column[j], j)
            r = 1.0 / d
            full = jnp.where(row != j, column[j], 0.0)
            low = jnp.where(row > j, column[j], 0.0)
            full_r = full * r
            lead = spread(factor_rows, j) * r
            for c in range(j + 1, 8):
                if c == j + 1:
                    column[c] = column[c] - (full * spread(column[c], j)) * r
                else:
                    column[c] = column[c] - full_r * spread(column[c], j)
            if more:
                right = [v - full_r * spread(v, j) for v in right]
            solved_rows = solved_rows - full * lead
            factor_rows = factor_rows - low * lead
            pivots = jnp.where(row == j, d, pivots)
            scale = jnp.where(row == j, r, scale)
        done.append(factor_rows * lax.rsqrt(pivots))
        if more:
            right = [v * scale for v in right]
            column = [below[c] - tree_sum(old[k, p + 1] * spread(right[c], k) for k in range(8)) for c in range(8)]
        solved_rows = solved_rows * scale
        heads = [spread(solved_rows, c) for c in range(8)]
        for g in range(p + 1, 8):
            a[g] = a[g] - tree_sum(old[c, g] * heads[c] for c in range(8))
    return jnp.concatenate(done, axis=0)[:, STEP:]


def factor_steps(a, e, block, half, cross, first):
    b, w = STEP, 128

    def upper(k):
        lo = k * w
        mid, hi = lo + b, lo + w
        t1 = half[...]
        inner = product(a[mid:hi, lo:mid], t1, NT)
        block[...] = a[mid:hi, mid:hi] - product(inner, inner, NT)
        e[lo:mid, lo:mid] = t1
        cross[...] = product(inner, t1, NN)

    def lower(k):
        lo = k * w
        mid, hi, nx = lo + b, lo + w, lo + 2 * w
        t2 = half[...]
        e[mid:hi, lo:mid] = -product(t2, cross[...], NN)
        e[mid:hi, mid:hi] = t2
        t = e[lo:hi, lo:hi]
        if hi < COUNT:
            below = product(a[hi:nx, lo:hi], t, NT)
            square = a[hi:nx, hi:nx] - product(below, below, NT)
            a[hi:nx, hi:nx] = square
            block[...] = square[:b, :b]
        if k > 0:
            left = product(t, e[lo:hi, :lo], NN)
            e[lo:hi, :lo] = left
        if hi < COUNT:
            if k > 0:
                e[hi:nx, :lo] = e[hi:nx, :lo] - product(below, left, NN)
            e[hi:nx, lo:hi] = -product(below, t, NN)
            if nx < COUNT:
                rest = product(a[nx:, lo:hi], t, NT)
                a[nx:, hi:nx] = a[nx:, hi:nx] - product(rest, below, NT)
                a[nx:, nx:] = a[nx:, nx:] - product(rest, rest, NT)
                if k > 0:
                    e[nx:, :lo] = e[nx:, :lo] - product(rest, left, NN)
                e[nx:, lo:hi] = -product(rest, t, NN)

    @pl.loop(0, 4)
    def _(i):
        half[...] = invert_factor(block[...])
        for n, (part, k) in enumerate(((upper, first), (lower, first), (upper, first + 1), (lower, first + 1))):
            pl.when(i == n)(lambda part=part, k=k: part(k))


STEPS_SCRATCH = [pltpu.VMEM((STEP, STEP), F32)] * 3


def factor_kernel(cov, own, near1, near2, near3, far, a, e, block, half, cross):
    _, _, y, c = place()
    for k in range(NY):
        for core in range(NC):
            piece = (own, near1, near2, near3)[k] if core == 0 else far.at[k]
            which = c if core == 0 else 1 - c
            first = pl.multiple_of(64 * which + 16 * lax.rem(y - k + NY, NY), 16)
            for b, (i, j) in enumerate(BLOCKS):
                at = (pl.ds(128 * i + first, 16), slice(128 * j, 128 * j + 128))
                a[at] = cov[at] - piece[16 * b : 16 * b + 16]
    e[...] = jnp.zeros_like(e)
    block[...] = a[:STEP, :STEP]
    factor_steps(a, e, block, half, cross, 0)


def factor(*args):
    square = jax.ShapeDtypeStruct((COUNT, COUNT), F32)
    return pl.pallas_call(
        factor_kernel,
        name="factor",
        out_shape=(square, square),
        in_specs=[VMEM] * 6,
        out_specs=(VMEM, VMEM),
        scratch_shapes=STEPS_SCRATCH,
        compiler_params=grant(10),
        cost_estimate=pl.CostEstimate(flops=10**10, bytes_accessed=4 << 20, transcendentals=0),
    )(*args)


def weights_kernel(a_in, e_in, sides, a, e, weights, block, half, cross):
    layer = lax.axis_index("layer")
    block[...] = a[256 : 256 + STEP, 256 : 256 + STEP]
    factor_steps(a, e, block, half, cross, 2)
    reduced = product(e[...], sides[:, :64].astype(F32), NN)
    weights[:64] = e[pl.ds(pl.multiple_of(64 * layer, 64), 64), :]
    weights[64:] = product(reduced, e[...], TN)


def weigh(a, e, sides):
    square = jax.ShapeDtypeStruct((COUNT, COUNT), F32)
    return pl.pallas_call(
        weights_kernel,
        name="weigh",
        out_shape=(square, square, jax.ShapeDtypeStruct((128, COUNT), F32)),
        in_specs=[VMEM] * 3,
        out_specs=(VMEM,) * 3,
        scratch_shapes=STEPS_SCRATCH,
        input_output_aliases={0: 0, 1: 1},
        compiler_params=grant(10),
        cost_estimate=pl.CostEstimate(flops=10**10, bytes_accessed=4 << 20, transcendentals=0),
    )(a, e, sides)[2]


def finish_kernel(weights, near, far, sides, panel, rest):
    _, _, y, c = place()
    up, low = upper_lower(weights[...])
    for piece, core in ((near, c), (far, 1 - c)):
        for k in range(NY):
            at = pl.multiple_of(512 * core + 128 * lax.rem(y - k + NY, NY), 128)
            both = halves_product(up, low, piece[k])
            panel[:, pl.ds(at, 128)] = both[:64]
            rest[:, pl.ds(at, 128)] = sides[:, pl.ds(at, 128)].astype(F32) - both[64:]


def finish(*args):
    return pl.pallas_call(
        finish_kernel,
        name="finish",
        out_shape=(jax.ShapeDtypeStruct((64, 1024), F32),) * 2,
        in_specs=[VMEM] * 4,
        out_specs=(VMEM, VMEM),
        compiler_params=grant(12),
        cost_estimate=pl.CostEstimate(flops=6 * 1024 * 512 * 128, bytes_accessed=3 << 20, transcendentals=0),
    )(*args)


def shards(window_points, pivot_points, window_factor, pivot_factor, right_sides, pivot_sides):
    _, _, y, c = place()
    swap = lambda a: lax.ppermute(a, "layer", SWAP)
    along = lambda a, k: lax.ppermute(a, "layer", shift_y(k))

    held = jnp.concatenate([pivot_factor, pivot_sides, jnp.zeros_like(pivot_sides)], axis=1)
    near = [held] + [lax.ppermute(held, "row", shift_x(k)) for k in (1, 2, 3)]
    pieces = tower(jnp.concatenate(near, axis=0))
    rows, sides, gram_other, gram_mine = gram(pieces)
    gram_far = swap(gram_other)
    gram_sum = [gram_mine[k] + gram_far[k] for k in range(NY)]
    gram_in = [along(gram_sum[k], k) for k in (1, 2, 3)]
    gram_own = gram_sum[0] + (gram_in[0] + gram_in[1] + gram_in[2])
    gram_near = [gram_own] + [along(gram_own, k) for k in (1, 2, 3)]
    gram_far = swap(jnp.stack(gram_near))

    points = lax.dynamic_slice_in_dim(window_points, 512 * c + 128 * y, 128, 1)
    cov = matern(pivot_points, pivot_points) + nugget_value * jnp.eye(COUNT, dtype=F32)
    covered = matern(points, pivot_points)
    cov, covered = lax.optimization_barrier((cov, covered))
    a, e = factor(cov, *gram_near, gram_far)
    weights = weigh(a, e, sides)

    schur_other, schur_mine = schur(window_factor, rows)
    schur_far = swap(schur_other)
    schur_sum = [schur_mine[k] + schur_far[k] for k in range(NY)]
    schur_in = [along(schur_sum[k], k) for k in (1, 2, 3)]
    panel_own = covered - (schur_sum[0] + (schur_in[0] + schur_in[1] + schur_in[2]))
    panel_near = jnp.stack([panel_own] + [along(panel_own, k) for k in (1, 2, 3)])
    panel_far = swap(panel_near)
    panel, rest = finish(weights, panel_near, panel_far, right_sides.T)
    return panel.T, rest.T


def solution(mesh):
    placed = (
        P(None, "row"),
        P(),
        P("row", "layer"),
        P("row", "layer"),
        P("row", "layer"),
        P("row", "layer"),
    )
    return jax.shard_map(
        shards,
        mesh=mesh,
        in_specs=placed,
        out_specs=(P("row", "layer"), P("row", "layer")),
        check_vma=False,
    )
```

```python
import jax
import jax.numpy as jnp
from jax import lax
from jax.experimental import pallas as pl
from jax.experimental.pallas import tpu as pltpu
from jax.sharding import PartitionSpec as P


nugget_value = 2.0
variance_value = 4.0
length_scale = 4.0


F32 = jnp.float32
BF16 = jnp.bfloat16
NN = ((1,), (0,))
NT = ((1,), (1,))
TN = ((0,), (0,))

NX, NZ, NY, NC = 4, 8, 4, 2
COUNT = 512
STEP = 64
BLOCKS = [(i, j) for i in range(4) for j in range(i + 1)]


def shift_x(k):
    return [(z * NX + x, z * NX + (x + k) % NX) for z in range(NZ) for x in range(NX)]


def shift_z(k):
    return [(z * NX + x, (z + k) % NZ * NX + x) for z in range(NZ) for x in range(NX)]


def shift_y(k):
    return [(y * NC + c, (y + k) % NY * NC + c) for y in range(NY) for c in range(NC)]


PAIRS = [[(y * NC + c, (y ^ 1 if n == 0 else NY - 1 - y) * NC + c) for y in range(NY) for c in range(NC)] for n in range(2)]
SWAP = [(y * NC + c, y * NC + 1 - c) for y in range(NY) for c in range(NC)]


def place():
    row, layer = lax.axis_index("row"), lax.axis_index("layer")
    return row // NX, lax.rem(row, NX), layer // NC, lax.rem(layer, NC)


def matern(first_points, second_points):
    first_float = first_points.astype(F32)
    second_float = second_points.astype(F32)
    delta_x = first_float[0][:, None] - second_float[0][None, :]
    delta_y = first_float[1][:, None] - second_float[1][None, :]
    scaled = jnp.sqrt(delta_x * delta_x + delta_y * delta_y) * (jnp.sqrt(3.0) / length_scale)
    return variance_value * (1.0 + scaled) * jnp.exp(-scaled)


def product(a, b, dims):
    return lax.dot_general(a, b, (dims, ((), ())), precision=lax.Precision.HIGHEST, preferred_element_type=F32)


def upper_lower(a):
    up = a.astype(BF16)
    return up, (a - up.astype(F32)).astype(BF16)


def halves_product(a_up, a_low, b):
    one = lambda u, v: lax.dot_general(u, v, (NT, ((), ())), preferred_element_type=F32)
    b_up, b_low = upper_lower(b)
    return one(a_low, b_up) + one(a_up, b_low) + one(a_up, b_up)


VMEM = pl.BlockSpec(memory_space=pltpu.VMEM)


def grant(mib):
    return pltpu.CompilerParams(vmem_limit_bytes=mib << 20)


PIECES = ((0, 0), (-1, 0), (1, 0), (-2, 0), (2, 0), (-3, 0), (3, 0), (4, 0), (4, 2))


def tower(own):
    hop = lambda a, k: lax.ppermute(a, "row", shift_z(k))
    up1, down1, up2, down2 = hop(own, 1), hop(own, -1), hop(own, 2), hop(own, -2)
    up3, down3 = hop(up2, 1), hop(down2, -1)
    up4, down4 = hop(up2[:32], 2), hop(down2[32:], -2)
    return [own, up1, down1, up2, down2, up3, down3, up4, down4]


def gram_kernel(*refs):
    pieces, (rows, sides, other, mine, blocks) = refs[:9], refs[9:]
    z, x, _, c = place()
    for piece, (turn, first) in zip(pieces, PIECES):

        @pl.loop(0, piece.shape[0] // 16)
        def _(i):
            at = (lax.rem(z + turn + NZ, NZ) * NX + lax.rem(x - first - i + NX, NX)) * 16
            at = pl.ds(pl.multiple_of(at, 16), 16)
            held = piece[pl.ds(pl.multiple_of(16 * i, 16), 16)]
            rows[at] = held[:, :2048]
            sides[at] = held[:, 2048:]

    at = 0
    for i in range(4):
        part = lax.dot_general(
            rows[128 * i : 128 * i + 128], rows[: 128 * i + 128], (NT, ((), ())), preferred_element_type=F32
        )
        for j in range(i + 1):
            blocks[at] = part[:, 128 * j : 128 * j + 128]
            at += 1
    for n in range(2):
        for out, core in ((other, 1 - c), (mine, c)):
            first = pl.multiple_of(64 * core + 32 * n, 32)
            for b in range(len(BLOCKS)):
                out[n, 32 * b : 32 * b + 32] = blocks[b, pl.ds(first, 32), :]


def gram(pieces):
    chunk = jax.ShapeDtypeStruct((2, 32 * len(BLOCKS), 128), F32)
    return pl.pallas_call(
        gram_kernel,
        name="gram",
        out_shape=(
            jax.ShapeDtypeStruct((COUNT, 2048), BF16),
            jax.ShapeDtypeStruct((COUNT, 128), BF16),
            chunk,
            chunk,
        ),
        in_specs=[VMEM] * 9,
        out_specs=(VMEM,) * 4,
        scratch_shapes=[pltpu.VMEM((len(BLOCKS), 128, 128), F32)],
        compiler_params=grant(10),
        cost_estimate=pl.CostEstimate(flops=2 * COUNT * COUNT * 2048, bytes_accessed=2 << 20, transcendentals=0),
    )(*pieces)


def schur_kernel(window, rows, other, mine, held, sem):
    _, _, y, c = place()

    def fetch(i):
        slot = lax.rem(i, 2)
        core = jnp.where(i < 2, 1 - c, c)
        first = pl.multiple_of(512 * core + 256 * slot, 256)
        return pltpu.make_async_copy(window.at[pl.ds(first, 256)], held.at[slot], sem.at[slot])

    fetch(0).start()

    @pl.loop(0, 4)
    def _(i):
        @pl.when(i < 3)
        def _():
            fetch(i + 1).start()

        fetch(i).wait()
        part = lax.dot_general(held[lax.rem(i, 2)], rows[...], (NT, ((), ())), preferred_element_type=F32)
        for n in range(2):
            k = lax.rem(2 * lax.rem(i, 2) + n - y + NY, NY)

            @pl.when(i < 2)
            def _():
                other[k] = part[128 * n : 128 * n + 128]

            @pl.when(i >= 2)
            def _():
                mine[k] = part[128 * n : 128 * n + 128]


def schur(window, rows):
    chunk = jax.ShapeDtypeStruct((NY, 128, COUNT), F32)
    return pl.pallas_call(
        schur_kernel,
        name="schur",
        out_shape=(chunk, chunk),
        in_specs=[pl.BlockSpec(memory_space=pltpu.HBM), VMEM],
        out_specs=(VMEM, VMEM),
        scratch_shapes=[pltpu.VMEM((2, 256, 2048), BF16), pltpu.SemaphoreType.DMA((2,))],
        compiler_params=grant(12),
        cost_estimate=pl.CostEstimate(flops=2 * 1024 * COUNT * 2048, bytes_accessed=8 << 20, transcendentals=0),
    )(window, rows)


def tree_sum(terms):
    terms = list(terms)
    while len(terms) > 1:
        terms = [terms[i] + terms[i + 1] if i + 1 < len(terms) else terms[i] for i in range(0, len(terms), 2)]
    return terms[0]


def invert_factor(block):
    lane = lax.broadcasted_iota(jnp.int32, (STEP, STEP), 1)
    sub = lax.broadcasted_iota(jnp.int32, (STEP, STEP), 0)
    both = jnp.concatenate([block, jnp.where(lane == sub, 1.0, 0.0).astype(F32)], axis=1)
    a = [both[8 * g : 8 * g + 8] for g in range(8)]
    row = lax.broadcasted_iota(jnp.int32, (8, 128), 0)
    spread = lambda v, j: jnp.broadcast_to(v[j : j + 1], (8, 128))
    lanes = lambda v, j: jnp.broadcast_to(v[:, j : j + 1], (8, 128))
    done = []
    column = [lanes(a[0], c) for c in range(8)]
    for p in range(8):
        more = p + 1 < 8
        if more:
            below = [lanes(a[p + 1], 8 * p + c) for c in range(8)]
            coming = [lanes(a[p + 1], 8 * p + 8 + c) for c in range(8)]
        old = {(c, g): lanes(a[g], 8 * p + c) for g in range(p + 2, 8) for c in range(8)}
        factor_rows = solved_rows = a[p]
        pivots = scale = jnp.ones((8, 128), F32)
        for j in range(8):
            d = spread(column[j], j)
            r = 1.0 / d
            full = jnp.where(row != j, column[j], 0.0)
            lead = spread(solved_rows, j)
            if j > 0:
                factor_rows = jnp.where(row == j, lead, factor_rows)
            pivots = jnp.where(row == j, d, pivots)
            scale = jnp.where(row == j, r, scale)
            heads = {c: spread(column[c], j) for c in range(j + 1, 8)}
            heads_r = {c: v * r for c, v in heads.items()}
            for c in range(j + 1, 8):
                column[c] = column[c] - ((full * heads[c]) * r if c == j + 1 else full * heads_r[c])
            solved_rows = solved_rows - full * (lead * r)
            if more:
                below_r = below[j] * r
                coming = [v - below_r * spread(below[j], c) for c, v in enumerate(coming)]
                a[p + 1] = a[p + 1] - below_r * lead
                for c in range(j + 1, 8):
                    below[c] = below[c] - below[j] * heads_r[c]
        done.append(factor_rows * lax.rsqrt(pivots))
        if more:
            column = coming
        if p + 2 < 8:
            solved_rows = solved_rows * scale
            leads = [spread(solved_rows, c) for c in range(8)]
            for g in range(p + 2, 8):
                a[g] = a[g] - tree_sum(old[c, g] * leads[c] for c in range(8))
    return jnp.concatenate(done, axis=0)[:, STEP:]


def factor_steps(a, e, block, half, cross, first):
    b, w = STEP, 128

    def upper(k):
        lo = k * w
        mid, hi = lo + b, lo + w
        t1 = half[...]
        inner = product(a[mid:hi, lo:mid], t1, NT)
        block[...] = a[mid:hi, mid:hi] - product(inner, inner, NT)
        e[lo:mid, lo:mid] = t1
        cross[...] = product(inner, t1, NN)

    def lower(k):
        lo = k * w
        mid, hi, nx = lo + b, lo + w, lo + 2 * w
        t2 = half[...]
        e[mid:hi, lo:mid] = -product(t2, cross[...], NN)
        e[mid:hi, mid:hi] = t2
        t = e[lo:hi, lo:hi]
        if hi < COUNT:
            below = product(a[hi:nx, lo:hi], t, NT)
            square = a[hi:nx, hi:nx] - product(below, below, NT)
            a[hi:nx, hi:nx] = square
            block[...] = square[:b, :b]
        if k > 0:
            left = product(t, e[lo:hi, :lo], NN)
            e[lo:hi, :lo] = left
        if hi < COUNT:
            if k > 0:
                e[hi:nx, :lo] = e[hi:nx, :lo] - product(below, left, NN)
            e[hi:nx, lo:hi] = -product(below, t, NN)
            if nx < COUNT:
                rest = product(a[nx:, lo:hi], t, NT)
                a[nx:, hi:nx] = a[nx:, hi:nx] - product(rest, below, NT)
                a[nx:, nx:] = a[nx:, nx:] - product(rest, rest, NT)
                if k > 0:
                    e[nx:, :lo] = e[nx:, :lo] - product(rest, left, NN)
                e[nx:, lo:hi] = -product(rest, t, NN)

    @pl.loop(0, 4)
    def _(i):
        half[...] = invert_factor(block[...])
        for n, (part, k) in enumerate(((upper, first), (lower, first), (upper, first + 1), (lower, first + 1))):
            pl.when(i == n)(lambda part=part, k=k: part(k))


STEPS_SCRATCH = [pltpu.VMEM((STEP, STEP), F32)] * 3


def factor_kernel(cov, near, far, a, e, block, half, cross):
    _, _, _, c = place()
    for n in range(2):
        for piece, core in ((near, c), (far, 1 - c)):
            first = pl.multiple_of(64 * core + 32 * n, 32)
            for b, (i, j) in enumerate(BLOCKS):
                at = (pl.ds(128 * i + first, 32), slice(128 * j, 128 * j + 128))
                a[at] = cov[at] - piece[n, 32 * b : 32 * b + 32]
    e[...] = jnp.zeros_like(e)
    block[...] = a[:STEP, :STEP]
    factor_steps(a, e, block, half, cross, 0)


def factor(*args):
    square = jax.ShapeDtypeStruct((COUNT, COUNT), F32)
    return pl.pallas_call(
        factor_kernel,
        name="factor",
        out_shape=(square, square),
        in_specs=[VMEM] * 3,
        out_specs=(VMEM, VMEM),
        scratch_shapes=STEPS_SCRATCH,
        compiler_params=grant(10),
        cost_estimate=pl.CostEstimate(flops=10**10, bytes_accessed=4 << 20, transcendentals=0),
    )(*args)


def weights_kernel(a_in, e_in, sides, a, e, weights, block, half, cross):
    layer = lax.axis_index("layer")
    block[...] = a[256 : 256 + STEP, 256 : 256 + STEP]
    factor_steps(a, e, block, half, cross, 2)
    reduced = product(e[...], sides[:, :64].astype(F32), NN)
    weights[:64] = e[pl.ds(pl.multiple_of(64 * layer, 64), 64), :]
    weights[64:] = product(reduced, e[...], TN)


def weigh(a, e, sides):
    square = jax.ShapeDtypeStruct((COUNT, COUNT), F32)
    return pl.pallas_call(
        weights_kernel,
        name="weigh",
        out_shape=(square, square, jax.ShapeDtypeStruct((128, COUNT), F32)),
        in_specs=[VMEM] * 3,
        out_specs=(VMEM,) * 3,
        scratch_shapes=STEPS_SCRATCH,
        input_output_aliases={0: 0, 1: 1},
        compiler_params=grant(10),
        cost_estimate=pl.CostEstimate(flops=10**10, bytes_accessed=4 << 20, transcendentals=0),
    )(a, e, sides)[2]


def finish_kernel(weights, near, far, sides, panel, rest):
    _, _, y, c = place()
    up, low = upper_lower(weights[...])
    for piece, core in ((near, c), (far, 1 - c)):
        for k in range(NY):
            at = pl.multiple_of(512 * core + 128 * lax.rem(y - k + NY, NY), 128)
            both = halves_product(up, low, piece[k])
            panel[:, pl.ds(at, 128)] = both[:64]
            rest[:, pl.ds(at, 128)] = sides[:, pl.ds(at, 128)].astype(F32) - both[64:]


def finish(*args):
    return pl.pallas_call(
        finish_kernel,
        name="finish",
        out_shape=(jax.ShapeDtypeStruct((64, 1024), F32),) * 2,
        in_specs=[VMEM] * 4,
        out_specs=(VMEM, VMEM),
        compiler_params=grant(12),
        cost_estimate=pl.CostEstimate(flops=6 * 1024 * 512 * 128, bytes_accessed=3 << 20, transcendentals=0),
    )(*args)


def shards(window_points, pivot_points, window_factor, pivot_factor, right_sides, pivot_sides):
    _, _, y, c = place()
    swap = lambda a: lax.ppermute(a, "layer", SWAP)
    along = lambda a, k: lax.ppermute(a, "layer", shift_y(k))

    held = jnp.concatenate([pivot_factor, pivot_sides, jnp.zeros_like(pivot_sides)], axis=1)
    near = [held] + [lax.ppermute(held, "row", shift_x(k)) for k in (1, 2, 3)]
    pieces = tower(jnp.concatenate(near, axis=0))
    rows, sides, gram_other, gram_mine = gram(pieces)
    gram_far = swap(gram_other)
    sums = [gram_mine[n] + gram_far[n] for n in range(2)]
    sums = [sums[n] + lax.ppermute(sums[n], "layer", PAIRS[n]) for n in range(2)]
    sums = [sums[n] + lax.ppermute(sums[n], "layer", PAIRS[1 - n]) for n in range(2)]
    gram_near = jnp.stack(sums)
    gram_far = swap(gram_near)

    points = lax.dynamic_slice_in_dim(window_points, 512 * c + 128 * y, 128, 1)
    cov = matern(pivot_points, pivot_points) + nugget_value * jnp.eye(COUNT, dtype=F32)
    covered = matern(points, pivot_points)
    cov, covered = lax.optimization_barrier((cov, covered))
    a, e = factor(cov, gram_near, gram_far)
    weights = weigh(a, e, sides)

    schur_other, schur_mine = schur(window_factor, rows)
    schur_far = swap(schur_other)
    schur_sum = [schur_mine[k] + schur_far[k] for k in range(NY)]
    schur_in = [along(schur_sum[k], k) for k in (1, 2, 3)]
    panel_own = covered - (schur_sum[0] + (schur_in[0] + schur_in[1] + schur_in[2]))
    panel_near = jnp.stack([panel_own] + [along(panel_own, k) for k in (1, 2, 3)])
    panel_far = swap(panel_near)
    panel, rest = finish(weights, panel_near, panel_far, right_sides.T)
    return panel.T, rest.T


def solution(mesh):
    placed = (
        P(None, "row"),
        P(),
        P("row", "layer"),
        P("row", "layer"),
        P("row", "layer"),
        P("row", "layer"),
    )
    return jax.shard_map(
        shards,
        mesh=mesh,
        in_specs=placed,
        out_specs=(P("row", "layer"), P("row", "layer")),
        check_vma=False,
    )
```

```python
import jax
import jax.numpy as jnp
from jax import lax
from jax.experimental import pallas as pl
from jax.experimental.pallas import tpu as pltpu
from jax.sharding import PartitionSpec as P


nugget_value = 2.0
variance_value = 4.0
length_scale = 4.0


F32 = jnp.float32
BF16 = jnp.bfloat16
NN = ((1,), (0,))
NT = ((1,), (1,))
TN = ((0,), (0,))

NX, NZ, NY, NC = 4, 8, 4, 2
COUNT = 512
STEP = 64
BLOCKS = [(i, j) for i in range(4) for j in range(i + 1)]


def shift_x(k):
    return [(z * NX + x, z * NX + (x + k) % NX) for z in range(NZ) for x in range(NX)]


def shift_z(k):
    return [(z * NX + x, (z + k) % NZ * NX + x) for z in range(NZ) for x in range(NX)]


def shift_y(k):
    return [(y * NC + c, (y + k) % NY * NC + c) for y in range(NY) for c in range(NC)]


PAIRS = [[(y * NC + c, (y ^ 1 if n == 0 else NY - 1 - y) * NC + c) for y in range(NY) for c in range(NC)] for n in range(2)]
SWAP = [(y * NC + c, y * NC + 1 - c) for y in range(NY) for c in range(NC)]


def place():
    row, layer = lax.axis_index("row"), lax.axis_index("layer")
    return row // NX, lax.rem(row, NX), layer // NC, lax.rem(layer, NC)


def matern(first_points, second_points):
    first_float = first_points.astype(F32)
    second_float = second_points.astype(F32)
    delta_x = first_float[0][:, None] - second_float[0][None, :]
    delta_y = first_float[1][:, None] - second_float[1][None, :]
    scaled = jnp.sqrt(delta_x * delta_x + delta_y * delta_y) * (jnp.sqrt(3.0) / length_scale)
    return variance_value * (1.0 + scaled) * jnp.exp(-scaled)


def product(a, b, dims):
    return lax.dot_general(a, b, (dims, ((), ())), precision=lax.Precision.HIGHEST, preferred_element_type=F32)


def upper_lower(a):
    up = a.astype(BF16)
    return up, (a - up.astype(F32)).astype(BF16)


def halves_product(a_up, a_low, b):
    one = lambda u, v: lax.dot_general(u, v, (NT, ((), ())), preferred_element_type=F32)
    b_up, b_low = upper_lower(b)
    return one(a_low, b_up) + one(a_up, b_low) + one(a_up, b_up)


VMEM = pl.BlockSpec(memory_space=pltpu.VMEM)


def grant(mib):
    return pltpu.CompilerParams(vmem_limit_bytes=mib << 20)


PIECES = ((0, 0), (-1, 0), (1, 0), (-2, 0), (2, 0), (-3, 0), (3, 0), (4, 0), (4, 2))


def tower(own):
    hop = lambda a, k: lax.ppermute(a, "row", shift_z(k))
    up1, down1, up2, down2 = hop(own, 1), hop(own, -1), hop(own, 2), hop(own, -2)
    up3, down3 = hop(up2, 1), hop(down2, -1)
    up4, down4 = hop(up2[:32], 2), hop(down2[32:], -2)
    return [own, up1, down1, up2, down2, up3, down3, up4, down4]


def sort_rows(pieces, places, rows, sides):
    z, x, _, _ = place()
    for piece, (turn, first) in zip(pieces, places):

        @pl.loop(0, piece.shape[0] // 16)
        def _(i):
            at = (lax.rem(z + turn + NZ, NZ) * NX + lax.rem(x - first - i + NX, NX)) * 16
            at = pl.ds(pl.multiple_of(at, 16), 16)
            held = piece[pl.ds(pl.multiple_of(16 * i, 16), 16)]
            rows[at] = held[:, :2048]
            sides[at] = held[:, 2048:]


SORTED = (jax.ShapeDtypeStruct((COUNT, 2048), BF16), jax.ShapeDtypeStruct((COUNT, 128), BF16))


def early_kernel(*refs):
    sort_rows(refs[:5], PIECES[:5], *refs[5:])


def early(pieces):
    return pl.pallas_call(
        early_kernel,
        name="early",
        out_shape=SORTED,
        in_specs=[VMEM] * 5,
        out_specs=(VMEM, VMEM),
        compiler_params=grant(4),
        cost_estimate=pl.CostEstimate(flops=10**6, bytes_accessed=2 << 20, transcendentals=0),
    )(*pieces)


def gram_kernel(rows_in, sides_in, up3, down3, up4, down4, rows, sides, other, mine, blocks):
    _, _, _, c = place()
    sort_rows((up3, down3, up4, down4), PIECES[5:], rows, sides)
    for half in range(2):
        part = lax.dot_general(
            rows[256 * half :], rows[256 * half : 256 * half + 256], (NT, ((), ())), preferred_element_type=F32
        )
        for b, (i, j) in enumerate(BLOCKS):
            if j // 2 == half:
                at = 128 * i - 256 * half
                blocks[b] = part[at : at + 128, 128 * (j % 2) : 128 * (j % 2) + 128]
    for n in range(2):
        for out, core in ((other, 1 - c), (mine, c)):
            first = pl.multiple_of(64 * core + 32 * n, 32)
            for b in range(len(BLOCKS)):
                out[n, 32 * b : 32 * b + 32] = blocks[b, pl.ds(first, 32), :]


def gram(rows, sides, pieces):
    chunk = jax.ShapeDtypeStruct((2, 32 * len(BLOCKS), 128), F32)
    return pl.pallas_call(
        gram_kernel,
        name="gram",
        out_shape=(*SORTED, chunk, chunk),
        in_specs=[VMEM] * 6,
        out_specs=(VMEM,) * 4,
        input_output_aliases={0: 0, 1: 1},
        scratch_shapes=[pltpu.VMEM((len(BLOCKS), 128, 128), F32)],
        compiler_params=grant(10),
        cost_estimate=pl.CostEstimate(flops=2 * COUNT * COUNT * 2048, bytes_accessed=2 << 20, transcendentals=0),
    )(rows, sides, *pieces)


def schur_kernel(window, rows, other, mine, held, sem):
    _, _, y, c = place()

    def fetch(i):
        core = 1 - c if i < 2 else c
        first = pl.multiple_of(512 * core + 256 * (i % 2), 256)
        return pltpu.make_async_copy(window.at[pl.ds(first, 256)], held.at[pl.ds(256 * i, 256)], sem.at[i])

    for i in range(4):
        fetch(i).start()
    for half, out in enumerate((other, mine)):
        for i in range(2):
            fetch(2 * half + i).wait()
        for n in range(2):
            part = lax.dot_general(
                held[512 * half : 512 * half + 512],
                rows[256 * n : 256 * n + 256],
                (NT, ((), ())),
                preferred_element_type=F32,
            )
            for i in range(NY):
                out[lax.rem(i - y + NY, NY), :, 256 * n : 256 * n + 256] = part[128 * i : 128 * i + 128]


def schur(window, rows):
    chunk = jax.ShapeDtypeStruct((NY, 128, COUNT), F32)
    return pl.pallas_call(
        schur_kernel,
        name="schur",
        out_shape=(chunk, chunk),
        in_specs=[pl.BlockSpec(memory_space=pltpu.HBM), VMEM],
        out_specs=(VMEM, VMEM),
        scratch_shapes=[pltpu.VMEM((1024, 2048), BF16), pltpu.SemaphoreType.DMA((4,))],
        compiler_params=grant(12),
        cost_estimate=pl.CostEstimate(flops=2 * 1024 * COUNT * 2048, bytes_accessed=8 << 20, transcendentals=0),
    )(window, rows)


def tree_sum(terms):
    terms = list(terms)
    while len(terms) > 1:
        terms = [terms[i] + terms[i + 1] if i + 1 < len(terms) else terms[i] for i in range(0, len(terms), 2)]
    return terms[0]


def invert_factor(block):
    lane = lax.broadcasted_iota(jnp.int32, (STEP, STEP), 1)
    sub = lax.broadcasted_iota(jnp.int32, (STEP, STEP), 0)
    both = jnp.concatenate([block, jnp.where(lane == sub, 1.0, 0.0).astype(F32)], axis=1)
    a = [both[8 * g : 8 * g + 8] for g in range(8)]
    row = lax.broadcasted_iota(jnp.int32, (8, 128), 0)
    spread = lambda v, j: jnp.broadcast_to(v[j : j + 1], (8, 128))
    lanes = lambda v, j: jnp.broadcast_to(v[:, j : j + 1], (8, 128))
    done = []
    column = [lanes(a[0], c) for c in range(8)]
    for p in range(8):
        more = p + 1 < 8
        if more:
            below = [lanes(a[p + 1], 8 * p + c) for c in range(8)]
            coming = [lanes(a[p + 1], 8 * p + 8 + c) for c in range(8)]
        old = {(c, g): lanes(a[g], 8 * p + c) for g in range(p + 2, 8) for c in range(8)}
        factor_rows = solved_rows = a[p]
        pivots = scale = jnp.ones((8, 128), F32)
        for j in range(8):
            d = spread(column[j], j)
            r = 1.0 / d
            full = jnp.where(row != j, column[j], 0.0)
            lead = spread(solved_rows, j)
            if j > 0:
                factor_rows = jnp.where(row == j, lead, factor_rows)
            pivots = jnp.where(row == j, d, pivots)
            scale = jnp.where(row == j, r, scale)
            heads = {c: spread(column[c], j) for c in range(j + 1, 8)}
            heads_r = {c: v * r for c, v in heads.items()}
            for c in range(j + 1, 8):
                column[c] = column[c] - ((full * heads[c]) * r if c == j + 1 else full * heads_r[c])
            solved_rows = solved_rows - full * (lead * r)
            if more:
                below_r = below[j] * r
                coming = [v - below_r * spread(below[j], c) for c, v in enumerate(coming)]
                a[p + 1] = a[p + 1] - below_r * lead
                for c in range(j + 1, 8):
                    below[c] = below[c] - below[j] * heads_r[c]
        done.append(factor_rows * lax.rsqrt(pivots))
        if more:
            column = coming
        if p + 2 < 8:
            solved_rows = solved_rows * scale
            leads = [spread(solved_rows, c) for c in range(8)]
            for g in range(p + 2, 8):
                a[g] = a[g] - tree_sum(old[c, g] * leads[c] for c in range(8))
    return jnp.concatenate(done, axis=0)[:, STEP:]


def factor_steps(a, e, block, half, cross, first):
    b, w = STEP, 128

    def upper(k):
        lo = k * w
        mid, hi = lo + b, lo + w
        t1 = half[...]
        inner = product(a[mid:hi, lo:mid], t1, NT)
        block[...] = a[mid:hi, mid:hi] - product(inner, inner, NT)
        e[lo:mid, lo:mid] = t1
        cross[...] = product(inner, t1, NN)

    def lower(k):
        lo = k * w
        mid, hi, nx = lo + b, lo + w, lo + 2 * w
        t2 = half[...]
        e[mid:hi, lo:mid] = -product(t2, cross[...], NN)
        e[mid:hi, mid:hi] = t2
        t = e[lo:hi, lo:hi]
        if hi < COUNT:
            below = product(a[hi:nx, lo:hi], t, NT)
            square = a[hi:nx, hi:nx] - product(below, below, NT)
            a[hi:nx, hi:nx] = square
            block[...] = square[:b, :b]
        if k > 0:
            left = product(t, e[lo:hi, :lo], NN)
            e[lo:hi, :lo] = left
        if hi < COUNT:
            if k > 0:
                e[hi:nx, :lo] = e[hi:nx, :lo] - product(below, left, NN)
            e[hi:nx, lo:hi] = -product(below, t, NN)
            if nx < COUNT:
                rest = product(a[nx:, lo:hi], t, NT)
                a[nx:, hi:nx] = a[nx:, hi:nx] - product(rest, below, NT)
                a[nx:, nx:] = a[nx:, nx:] - product(rest, rest, NT)
                if k > 0:
                    e[nx:, :lo] = e[nx:, :lo] - product(rest, left, NN)
                e[nx:, lo:hi] = -product(rest, t, NN)

    @pl.loop(0, 4)
    def _(i):
        half[...] = invert_factor(block[...])
        for n, (part, k) in enumerate(((upper, first), (lower, first), (upper, first + 1), (lower, first + 1))):
            pl.when(i == n)(lambda part=part, k=k: part(k))


STEPS_SCRATCH = [pltpu.VMEM((STEP, STEP), F32)] * 3


def factor_kernel(cov, near, far, a, e, block, half, cross):
    _, _, _, c = place()
    for n in range(2):
        for piece, core in ((near, c), (far, 1 - c)):
            first = pl.multiple_of(64 * core + 32 * n, 32)
            for b, (i, j) in enumerate(BLOCKS):
                at = (pl.ds(128 * i + first, 32), slice(128 * j, 128 * j + 128))
                a[at] = cov[at] - piece[n, 32 * b : 32 * b + 32]
    e[...] = jnp.zeros_like(e)
    block[...] = a[:STEP, :STEP]
    factor_steps(a, e, block, half, cross, 0)


def factor(*args):
    square = jax.ShapeDtypeStruct((COUNT, COUNT), F32)
    return pl.pallas_call(
        factor_kernel,
        name="factor",
        out_shape=(square, square),
        in_specs=[VMEM] * 3,
        out_specs=(VMEM, VMEM),
        scratch_shapes=STEPS_SCRATCH,
        compiler_params=grant(10),
        cost_estimate=pl.CostEstimate(flops=10**10, bytes_accessed=4 << 20, transcendentals=0),
    )(*args)


def weights_kernel(a_in, e_in, sides, a, e, weights, block, half, cross):
    layer = lax.axis_index("layer")
    block[...] = a[256 : 256 + STEP, 256 : 256 + STEP]
    factor_steps(a, e, block, half, cross, 2)
    reduced = product(e[...], sides[:, :64].astype(F32), NN)
    weights[:64] = e[pl.ds(pl.multiple_of(64 * layer, 64), 64), :]
    weights[64:] = product(reduced, e[...], TN)


def weigh(a, e, sides):
    square = jax.ShapeDtypeStruct((COUNT, COUNT), F32)
    return pl.pallas_call(
        weights_kernel,
        name="weigh",
        out_shape=(square, square, jax.ShapeDtypeStruct((128, COUNT), F32)),
        in_specs=[VMEM] * 3,
        out_specs=(VMEM,) * 3,
        scratch_shapes=STEPS_SCRATCH,
        input_output_aliases={0: 0, 1: 1},
        compiler_params=grant(10),
        cost_estimate=pl.CostEstimate(flops=10**10, bytes_accessed=4 << 20, transcendentals=0),
    )(a, e, sides)[2]


def finish_kernel(weights, near, far, sides, panel, rest):
    _, _, y, c = place()
    up, low = upper_lower(weights[...])
    for piece, core in ((near, c), (far, 1 - c)):
        for k in range(NY):
            at = pl.multiple_of(512 * core + 128 * lax.rem(y - k + NY, NY), 128)
            both = halves_product(up, low, piece[k])
            panel[:, pl.ds(at, 128)] = both[:64]
            rest[:, pl.ds(at, 128)] = sides[:, pl.ds(at, 128)].astype(F32) - both[64:]


def finish(*args):
    return pl.pallas_call(
        finish_kernel,
        name="finish",
        out_shape=(jax.ShapeDtypeStruct((64, 1024), F32),) * 2,
        in_specs=[VMEM] * 4,
        out_specs=(VMEM, VMEM),
        compiler_params=grant(12),
        cost_estimate=pl.CostEstimate(flops=6 * 1024 * 512 * 128, bytes_accessed=3 << 20, transcendentals=0),
    )(*args)


def shards(window_points, pivot_points, window_factor, pivot_factor, right_sides, pivot_sides):
    _, _, y, c = place()
    swap = lambda a: lax.ppermute(a, "layer", SWAP)
    along = lambda a, k: lax.ppermute(a, "layer", shift_y(k))

    held = jnp.concatenate([pivot_factor, pivot_sides, jnp.zeros_like(pivot_sides)], axis=1)
    near = [held] + [lax.ppermute(held, "row", shift_x(k)) for k in (1, 2, 3)]
    pieces = tower(jnp.concatenate(near, axis=0))
    rows, sides, gram_other, gram_mine = gram(*early(pieces[:5]), pieces[5:])
    gram_far = swap(gram_other)
    sums = [gram_mine[n] + gram_far[n] for n in range(2)]
    sums = [sums[n] + lax.ppermute(sums[n], "layer", PAIRS[n]) for n in range(2)]
    sums = [sums[n] + lax.ppermute(sums[n], "layer", PAIRS[1 - n]) for n in range(2)]
    gram_near = jnp.stack(sums)
    gram_far = swap(gram_near)

    points = lax.dynamic_slice_in_dim(window_points, 512 * c + 128 * y, 128, 1)
    cov = matern(pivot_points, pivot_points) + nugget_value * jnp.eye(COUNT, dtype=F32)
    covered = matern(points, pivot_points)
    cov, covered = lax.optimization_barrier((cov, covered))
    a, e = factor(cov, gram_near, gram_far)
    weights = weigh(a, e, sides)

    schur_other, schur_mine = schur(window_factor, rows)
    schur_far = swap(schur_other)
    schur_sum = [schur_mine[k] + schur_far[k] for k in range(NY)]
    schur_in = [along(schur_sum[k], k) for k in (1, 2, 3)]
    panel_own = covered - (schur_sum[0] + (schur_in[0] + schur_in[1] + schur_in[2]))
    panel_near = jnp.stack([panel_own] + [along(panel_own, k) for k in (1, 2, 3)])
    panel_far = swap(panel_near)
    panel, rest = finish(weights, panel_near, panel_far, right_sides.T)
    return panel.T, rest.T


def solution(mesh):
    placed = (
        P(None, "row"),
        P(),
        P("row", "layer"),
        P("row", "layer"),
        P("row", "layer"),
        P("row", "layer"),
    )
    return jax.shard_map(
        shards,
        mesh=mesh,
        in_specs=placed,
        out_specs=(P("row", "layer"), P("row", "layer")),
        check_vma=False,
    )
```

```python
import jax
import jax.numpy as jnp
from jax import lax
from jax.experimental import pallas as pl
from jax.experimental.pallas import tpu as pltpu
from jax.sharding import PartitionSpec as P


nugget_value = 2.0
variance_value = 4.0
length_scale = 4.0


F32 = jnp.float32
BF16 = jnp.bfloat16
NN = ((1,), (0,))
NT = ((1,), (1,))
TN = ((0,), (0,))

NX, NZ, NY, NC = 4, 8, 4, 2
COUNT = 512
STEP = 64
BLOCKS = [(i, j) for i in range(4) for j in range(i + 1)]


def shift_x(k):
    return [(z * NX + x, z * NX + (x + k) % NX) for z in range(NZ) for x in range(NX)]


def shift_z(k):
    return [(z * NX + x, (z + k) % NZ * NX + x) for z in range(NZ) for x in range(NX)]


def shift_y(k):
    return [(y * NC + c, (y + k) % NY * NC + c) for y in range(NY) for c in range(NC)]


PAIRS = [[(y * NC + c, (y ^ 1 if n == 0 else NY - 1 - y) * NC + c) for y in range(NY) for c in range(NC)] for n in range(2)]
SWAP = [(y * NC + c, y * NC + 1 - c) for y in range(NY) for c in range(NC)]


def place():
    row, layer = lax.axis_index("row"), lax.axis_index("layer")
    return row // NX, lax.rem(row, NX), layer // NC, lax.rem(layer, NC)


def matern(first_points, second_points):
    first_float = first_points.astype(F32)
    second_float = second_points.astype(F32)
    delta_x = first_float[0][:, None] - second_float[0][None, :]
    delta_y = first_float[1][:, None] - second_float[1][None, :]
    scaled = jnp.sqrt(delta_x * delta_x + delta_y * delta_y) * (jnp.sqrt(3.0) / length_scale)
    return variance_value * (1.0 + scaled) * jnp.exp(-scaled)


def product(a, b, dims):
    return lax.dot_general(a, b, (dims, ((), ())), precision=lax.Precision.HIGHEST, preferred_element_type=F32)


def upper_lower(a):
    up = a.astype(BF16)
    return up, (a - up.astype(F32)).astype(BF16)


def halves_product(a_up, a_low, b):
    one = lambda u, v: lax.dot_general(u, v, (NT, ((), ())), preferred_element_type=F32)
    b_up, b_low = upper_lower(b)
    return one(a_low, b_up) + one(a_up, b_low) + one(a_up, b_up)


LEFT = 1024
HELD = LEFT + 128
PART = 256
VMEM = pl.BlockSpec(memory_space=pltpu.VMEM)


def grant(mib):
    return pltpu.CompilerParams(vmem_limit_bytes=mib << 20)


PIECES = ((0, 0), (-1, 0), (1, 0), (-2, 0), (2, 0), (-3, 0), (3, 0), (4, 0), (4, 2))


def tower(own):
    hop = lambda a, k: lax.ppermute(a, "row", shift_z(k))
    up1, down1, up2, down2 = hop(own, 1), hop(own, -1), hop(own, 2), hop(own, -2)
    up3, down3 = hop(up2, 1), hop(down2, -1)
    up4, down4 = hop(up2[:32], 2), hop(down2[32:], -2)
    return [own, up1, down1, up2, down2, up3, down3, up4, down4]


def kernel_call(body, out_shape, mib, *args, aliases={}, scratch=()):
    return pl.pallas_call(
        body,
        out_shape=out_shape,
        in_specs=[VMEM] * len(args),
        out_specs=jax.tree.map(lambda a: VMEM, out_shape),
        input_output_aliases=aliases,
        scratch_shapes=scratch,
        compiler_params=grant(mib),
        cost_estimate=pl.CostEstimate(flops=10**6, bytes_accessed=1 << 20, transcendentals=0),
    )(*args)


def prepare_kernel(factor_rows, sides, held, right):
    held[:, :LEFT] = factor_rows[:, :LEFT]
    held[:, LEFT:] = jnp.concatenate([sides[...], jnp.zeros_like(sides)], axis=1)
    for i in range(4):
        right[16 * i : 16 * i + 16] = factor_rows[:, LEFT + PART * i : LEFT + PART * i + PART]


def pack_kernel(near0, near1, near2, near3, right, out):
    for i, piece in enumerate((near0, near1, near2, near3)):
        out[16 * i : 16 * i + 16, :HELD] = piece[...]
    out[:, HELD:] = right[...]


def take_kernel(*refs):
    at = 0
    for piece in refs[:-1]:
        size = piece.shape[0]
        refs[-1][at : at + size] = piece[:, HELD:]
        at += size


def row_of(z, x):
    return pl.ds(pl.multiple_of((lax.rem(z + NZ, NZ) * NX + lax.rem(x + NX, NX)) * 16, 16), 16)


def sort_left(pieces, places, rows, sides):
    z, x, _, _ = place()
    for piece, (turn, first) in zip(pieces, places):

        @pl.loop(0, piece.shape[0] // 16)
        def _(i):
            at = row_of(z + turn, x - first - i)
            held = piece[pl.ds(pl.multiple_of(16 * i, 16), 16)]
            rows[at, :LEFT] = held[:, :LEFT]
            sides[at] = held[:, LEFT:HELD]


def sort_right(pieces, turns, rows):
    z, x, _, _ = place()
    for k, piece in enumerate(pieces):
        for n, turn in enumerate(turns):
            for q in range(4):
                first = 64 * n + 16 * q
                rows[row_of(z + turn, x - k), LEFT + PART * q : LEFT + PART * q + PART] = piece[first : first + 16]


SORTED = (jax.ShapeDtypeStruct((COUNT, 2048), BF16), jax.ShapeDtypeStruct((COUNT, 128), BF16))


def early_kernel(*refs):
    sort_left(refs[:5], PIECES[:5], *refs[5:])


def gram_kernel(*refs):
    pieces, first, second, (rows, sides, other, mine, blocks) = refs[2:6], refs[6:10], refs[10:14], refs[14:]
    _, _, _, c = place()
    sort_left(pieces, PIECES[5:], rows, sides)
    sort_right(first, (0, -1, 1, -2, 2), rows)
    sort_right(second, (-3, 3, 4), rows)
    for half in range(2):
        part = lax.dot_general(
            rows[256 * half :], rows[256 * half : 256 * half + 256], (NT, ((), ())), preferred_element_type=F32
        )
        for b, (i, j) in enumerate(BLOCKS):
            if j // 2 == half:
                at = 128 * i - 256 * half
                blocks[b] = part[at : at + 128, 128 * (j % 2) : 128 * (j % 2) + 128]
    for n in range(2):
        for out, core in ((other, 1 - c), (mine, c)):
            first = pl.multiple_of(64 * core + 32 * n, 32)
            for b in range(len(BLOCKS)):
                out[n, 32 * b : 32 * b + 32] = blocks[b, pl.ds(first, 32), :]


def gram(*args):
    chunk = jax.ShapeDtypeStruct((2, 32 * len(BLOCKS), 128), F32)
    scratch = [pltpu.VMEM((len(BLOCKS), 128, 128), F32)]
    return kernel_call(gram_kernel, (*SORTED, chunk, chunk), 10, *args, aliases={0: 0, 1: 1}, scratch=scratch)


def schur_kernel(window, rows, other, mine, held, sem):
    _, _, y, c = place()

    def fetch(i):
        core = 1 - c if i < 2 else c
        first = pl.multiple_of(512 * core + 256 * (i % 2), 256)
        return pltpu.make_async_copy(window.at[pl.ds(first, 256)], held.at[pl.ds(256 * i, 256)], sem.at[i])

    for i in range(4):
        fetch(i).start()
    for half, out in enumerate((other, mine)):
        for i in range(2):
            fetch(2 * half + i).wait()
        for n in range(2):
            part = lax.dot_general(
                held[512 * half : 512 * half + 512],
                rows[256 * n : 256 * n + 256],
                (NT, ((), ())),
                preferred_element_type=F32,
            )
            for i in range(NY):
                out[lax.rem(i - y + NY, NY), :, 256 * n : 256 * n + 256] = part[128 * i : 128 * i + 128]


def schur(window, rows):
    chunk = jax.ShapeDtypeStruct((NY, 128, COUNT), F32)
    return pl.pallas_call(
        schur_kernel,
        name="schur",
        out_shape=(chunk, chunk),
        in_specs=[pl.BlockSpec(memory_space=pltpu.HBM), VMEM],
        out_specs=(VMEM, VMEM),
        scratch_shapes=[pltpu.VMEM((1024, 2048), BF16), pltpu.SemaphoreType.DMA((4,))],
        compiler_params=grant(12),
        cost_estimate=pl.CostEstimate(flops=2 * 1024 * COUNT * 2048, bytes_accessed=8 << 20, transcendentals=0),
    )(window, rows)


def tree_sum(terms):
    terms = list(terms)
    while len(terms) > 1:
        terms = [terms[i] + terms[i + 1] if i + 1 < len(terms) else terms[i] for i in range(0, len(terms), 2)]
    return terms[0]


def invert_factor(block):
    lane = lax.broadcasted_iota(jnp.int32, (STEP, STEP), 1)
    sub = lax.broadcasted_iota(jnp.int32, (STEP, STEP), 0)
    both = jnp.concatenate([block, jnp.where(lane == sub, 1.0, 0.0).astype(F32)], axis=1)
    a = [both[8 * g : 8 * g + 8] for g in range(8)]
    row = lax.broadcasted_iota(jnp.int32, (8, 128), 0)
    spread = lambda v, j: jnp.broadcast_to(v[j : j + 1], (8, 128))
    lanes = lambda v, j: jnp.broadcast_to(v[:, j : j + 1], (8, 128))
    done = []
    column = [lanes(a[0], c) for c in range(8)]
    for p in range(8):
        more = p + 1 < 8
        if more:
            below = [lanes(a[p + 1], 8 * p + c) for c in range(8)]
            coming = [lanes(a[p + 1], 8 * p + 8 + c) for c in range(8)]
        old = {(c, g): lanes(a[g], 8 * p + c) for g in range(p + 2, 8) for c in range(8)}
        factor_rows = solved_rows = a[p]
        pivots = scale = jnp.ones((8, 128), F32)
        for j in range(8):
            d = spread(column[j], j)
            r = 1.0 / d
            full = jnp.where(row != j, column[j], 0.0)
            lead = spread(solved_rows, j)
            if j > 0:
                factor_rows = jnp.where(row == j, lead, factor_rows)
            pivots = jnp.where(row == j, d, pivots)
            scale = jnp.where(row == j, r, scale)
            heads = {c: spread(column[c], j) for c in range(j + 1, 8)}
            heads_r = {c: v * r for c, v in heads.items()}
            for c in range(j + 1, 8):
                column[c] = column[c] - ((full * heads[c]) * r if c == j + 1 else full * heads_r[c])
            solved_rows = solved_rows - full * (lead * r)
            if more:
                below_r = below[j] * r
                coming = [v - below_r * spread(below[j], c) for c, v in enumerate(coming)]
                a[p + 1] = a[p + 1] - below_r * lead
                for c in range(j + 1, 8):
                    below[c] = below[c] - below[j] * heads_r[c]
        done.append(factor_rows * lax.rsqrt(pivots))
        if more:
            column = coming
        if p + 2 < 8:
            solved_rows = solved_rows * scale
            leads = [spread(solved_rows, c) for c in range(8)]
            for g in range(p + 2, 8):
                a[g] = a[g] - tree_sum(old[c, g] * leads[c] for c in range(8))
    return jnp.concatenate(done, axis=0)[:, STEP:]


def factor_steps(a, e, block, half, cross, first):
    b, w = STEP, 128

    def upper(k):
        lo = k * w
        mid, hi = lo + b, lo + w
        t1 = half[...]
        inner = product(a[mid:hi, lo:mid], t1, NT)
        block[...] = a[mid:hi, mid:hi] - product(inner, inner, NT)
        e[lo:mid, lo:mid] = t1
        cross[...] = product(inner, t1, NN)

    def lower(k):
        lo = k * w
        mid, hi, nx = lo + b, lo + w, lo + 2 * w
        t2 = half[...]
        e[mid:hi, lo:mid] = -product(t2, cross[...], NN)
        e[mid:hi, mid:hi] = t2
        t = e[lo:hi, lo:hi]
        if hi < COUNT:
            below = product(a[hi:nx, lo:hi], t, NT)
            square = a[hi:nx, hi:nx] - product(below, below, NT)
            a[hi:nx, hi:nx] = square
            block[...] = square[:b, :b]
        if k > 0:
            left = product(t, e[lo:hi, :lo], NN)
            e[lo:hi, :lo] = left
        if hi < COUNT:
            if k > 0:
                e[hi:nx, :lo] = e[hi:nx, :lo] - product(below, left, NN)
            e[hi:nx, lo:hi] = -product(below, t, NN)
            if nx < COUNT:
                rest = product(a[nx:, lo:hi], t, NT)
                a[nx:, hi:nx] = a[nx:, hi:nx] - product(rest, below, NT)
                a[nx:, nx:] = a[nx:, nx:] - product(rest, rest, NT)
                if k > 0:
                    e[nx:, :lo] = e[nx:, :lo] - product(rest, left, NN)
                e[nx:, lo:hi] = -product(rest, t, NN)

    @pl.loop(0, 4)
    def _(i):
        half[...] = invert_factor(block[...])
        for n, (part, k) in enumerate(((upper, first), (lower, first), (upper, first + 1), (lower, first + 1))):
            pl.when(i == n)(lambda part=part, k=k: part(k))


STEPS_SCRATCH = [pltpu.VMEM((STEP, STEP), F32)] * 3


def factor_kernel(cov, near, far, a, e, block, half, cross):
    _, _, _, c = place()
    for n in range(2):
        for piece, core in ((near, c), (far, 1 - c)):
            first = pl.multiple_of(64 * core + 32 * n, 32)
            for b, (i, j) in enumerate(BLOCKS):
                at = (pl.ds(128 * i + first, 32), slice(128 * j, 128 * j + 128))
                a[at] = cov[at] - piece[n, 32 * b : 32 * b + 32]
    e[...] = jnp.zeros_like(e)
    block[...] = a[:STEP, :STEP]
    factor_steps(a, e, block, half, cross, 0)


def factor(*args):
    square = jax.ShapeDtypeStruct((COUNT, COUNT), F32)
    return pl.pallas_call(
        factor_kernel,
        name="factor",
        out_shape=(square, square),
        in_specs=[VMEM] * 3,
        out_specs=(VMEM, VMEM),
        scratch_shapes=STEPS_SCRATCH,
        compiler_params=grant(10),
        cost_estimate=pl.CostEstimate(flops=10**10, bytes_accessed=4 << 20, transcendentals=0),
    )(*args)


def weights_kernel(a_in, e_in, sides, a, e, weights, block, half, cross):
    layer = lax.axis_index("layer")
    block[...] = a[256 : 256 + STEP, 256 : 256 + STEP]
    factor_steps(a, e, block, half, cross, 2)
    reduced = product(e[...], sides[:, :64].astype(F32), NN)
    weights[:64] = e[pl.ds(pl.multiple_of(64 * layer, 64), 64), :]
    weights[64:] = product(reduced, e[...], TN)


def weigh(a, e, sides):
    square = jax.ShapeDtypeStruct((COUNT, COUNT), F32)
    return pl.pallas_call(
        weights_kernel,
        name="weigh",
        out_shape=(square, square, jax.ShapeDtypeStruct((128, COUNT), F32)),
        in_specs=[VMEM] * 3,
        out_specs=(VMEM,) * 3,
        scratch_shapes=STEPS_SCRATCH,
        input_output_aliases={0: 0, 1: 1},
        compiler_params=grant(10),
        cost_estimate=pl.CostEstimate(flops=10**10, bytes_accessed=4 << 20, transcendentals=0),
    )(a, e, sides)[2]


def finish_kernel(weights, near, far, sides, panel, rest):
    _, _, y, c = place()
    up, low = upper_lower(weights[...])
    for piece, core in ((near, c), (far, 1 - c)):
        for k in range(NY):
            at = pl.multiple_of(512 * core + 128 * lax.rem(y - k + NY, NY), 128)
            both = halves_product(up, low, piece[k])
            panel[:, pl.ds(at, 128)] = both[:64]
            rest[:, pl.ds(at, 128)] = sides[:, pl.ds(at, 128)].astype(F32) - both[64:]


def finish(*args):
    return pl.pallas_call(
        finish_kernel,
        name="finish",
        out_shape=(jax.ShapeDtypeStruct((64, 1024), F32),) * 2,
        in_specs=[VMEM] * 4,
        out_specs=(VMEM, VMEM),
        compiler_params=grant(12),
        cost_estimate=pl.CostEstimate(flops=6 * 1024 * 512 * 128, bytes_accessed=3 << 20, transcendentals=0),
    )(*args)


def shards(window_points, pivot_points, window_factor, pivot_factor, right_sides, pivot_sides):
    _, _, y, c = place()
    swap = lambda a: lax.ppermute(a, "layer", SWAP)
    along = lambda a, k: lax.ppermute(a, "layer", shift_y(k))

    over_x = lambda a: [a] + [lax.ppermute(a, "row", shift_x(k)) for k in (1, 2, 3)]
    take = lambda pieces: kernel_call(
        take_kernel, jax.ShapeDtypeStruct((sum(a.shape[0] for a in pieces), PART), BF16), 2, *pieces
    )

    shapes = (jax.ShapeDtypeStruct((16, HELD), BF16), jax.ShapeDtypeStruct((64, PART), BF16))
    held, right = kernel_call(prepare_kernel, shapes, 1, pivot_factor, pivot_sides)
    packed = jax.ShapeDtypeStruct((64, HELD + PART), BF16)
    pieces = tower(kernel_call(pack_kernel, packed, 2, *over_x(held), right))
    first = over_x(take(pieces[:5]))
    sorted_rows = kernel_call(early_kernel, SORTED, 4, *pieces[:5])
    second = over_x(take(pieces[5:]))
    rows, sides, gram_other, gram_mine = gram(*sorted_rows, *pieces[5:], *first, *second)

    gram_far = swap(gram_other)
    sums = [gram_mine[n] + gram_far[n] for n in range(2)]
    sums = [sums[n] + lax.ppermute(sums[n], "layer", PAIRS[n]) for n in range(2)]
    sums = [sums[n] + lax.ppermute(sums[n], "layer", PAIRS[1 - n]) for n in range(2)]
    gram_near = jnp.stack(sums)
    gram_far = swap(gram_near)

    points = lax.dynamic_slice_in_dim(window_points, 512 * c + 128 * y, 128, 1)
    cov = matern(pivot_points, pivot_points) + nugget_value * jnp.eye(COUNT, dtype=F32)
    covered = matern(points, pivot_points)
    cov, covered = lax.optimization_barrier((cov, covered))
    a, e = factor(cov, gram_near, gram_far)
    weights = weigh(a, e, sides)

    schur_other, schur_mine = schur(window_factor, rows)
    schur_far = swap(schur_other)
    schur_sum = [schur_mine[k] + schur_far[k] for k in range(NY)]
    schur_in = [along(schur_sum[k], k) for k in (1, 2, 3)]
    panel_own = covered - (schur_sum[0] + (schur_in[0] + schur_in[1] + schur_in[2]))
    panel_near = jnp.stack([panel_own] + [along(panel_own, k) for k in (1, 2, 3)])
    panel_far = swap(panel_near)
    panel, rest = finish(weights, panel_near, panel_far, right_sides.T)
    return panel.T, rest.T


def solution(mesh):
    placed = (
        P(None, "row"),
        P(),
        P("row", "layer"),
        P("row", "layer"),
        P("row", "layer"),
        P("row", "layer"),
    )
    return jax.shard_map(
        shards,
        mesh=mesh,
        in_specs=placed,
        out_specs=(P("row", "layer"), P("row", "layer")),
        check_vma=False,
    )
```
